32 devices in a mesh: obs: 8 (over z, y), rep: 4 (over x, core).
Axes of the slice: x: 2, y: 2, z: 4, core: 2. Of those that a mesh axis runs over, the one named last changes fastest.
Arguments:
- jacobians: float32 [18, 131072], P(None, ('obs', 'rep')), may hold values from -3 to 3
- residuals: float32 [2, 131072], P(None, ('obs', 'rep')), may hold values from -6 to 6
- camera_local: int32 [131072], P(('obs', 'rep')), may hold values from 0 to 1023
- bucket_counts: int32 [32, 8], P(('obs', 'rep')), may hold values from 1 to 512, as said below
- camera_map: int32 [8192], replicated, may hold values from 0 to 8191, each once
Outputs:
- gradient: float32 [9, 8192], replicated
- camera_blocks: float32 [81, 8192], P(None, 'obs')
The draws below stay inside these ranges and needn't reach their ends.
Inputs may be any that keep to these rules, and one draw needn't show every extreme that they name: bucket_counts[s, d] counts the leading live slots of bucket d of source block s; exactly one destination d has all 512 slots live from every source block, and every other bucket has at most 256 live slots. A slot in bucket d names camera slot d * 1024 + camera_local. `camera_map`: each camera id appears once.
All inputs are finite; a program needn't handle non-finite values.
Results may differ from the reference program's by a relative error of at most 0.0003.
Values sent between devices are 32-bit elements; how exact they have to be, the bound alone decides.
A program may use at most 192 MiB of HBM per device.

```python
import math
import jax
import jax.numpy as jnp
import numpy as np
from jax import lax

CAM_DEV = 1024
CAP = 512
CAM = 8192
SLOTS = 131072
N_OBS = 8
N_REP = 4


def draw_bucket_counts(key, part):
    key_hot = jax.random.fold_in(key, 11)
    key_full = jax.random.fold_in(key, 12)
    key_base = jax.random.fold_in(key, 13)
    hotness = jax.random.randint(key_hot, (N_OBS,), 1, 4)
    full_column = jax.random.randint(key_full, (), 0, N_OBS)
    baseline = jax.random.randint(key_base, (N_OBS * N_REP, N_OBS), CAP // 4, CAP // 2 + 1)
    counts = jnp.minimum(CAP // 2, baseline * hotness[None, :] // 2)
    counts = jnp.maximum(counts, 1)
    column_ids = jnp.arange(N_OBS, dtype=jnp.int32)
    counts = jnp.where(column_ids[None, :] == full_column, CAP, counts)
    return counts.astype(jnp.int32)


def set_ends(drawn, rng, low, largest):
    index_at = [jax.random.randint(jax.random.fold_in(rng, axis), (), 0, length) for axis, length in enumerate(drawn.shape)]
    widest = drawn.shape.index(max(drawn.shape))
    neighbour = index_at[:widest] + [(index_at[widest] + 1) % drawn.shape[widest]] + index_at[widest + 1:]
    return drawn.at[tuple(index_at)].set(low).at[tuple(neighbour)].set(largest)


def block_scale(rng, dims, pieces, smallest, high):
    level, own = 1.0, jax.random.fold_in(rng, 6)
    for dim, shards_of in pieces:
        heights = jnp.exp(jax.random.uniform(jax.random.fold_in(own, dim), (shards_of,), jnp.float32, smallest / len(pieces), high / len(pieces)))
        level = level * jnp.repeat(heights, dims[dim] // shards_of).reshape([-1 if axis == dim else 1 for axis in range(len(dims))])
    return level


def rank_bounds(amount, skew):
    loads = [(1 << 20) // math.isqrt(grade ** skew) + 1 for grade in range(1, amount + 1)]
    scale = 1 + sum(loads) // (1 << 30)
    return np.cumsum(np.array([max(1, weight // scale) for weight in loads]))


def ranked_ids(key, dims, count, lean):
    grid = rank_bounds(count, lean)
    ticket = jax.random.randint(jax.random.fold_in(key, 1), dims, 0, int(grid[count - 1]))
    grade = jnp.searchsorted(jnp.asarray(grid, jnp.int32), ticket, side="right")
    return jax.random.permutation(jax.random.fold_in(key, 2), count)[grade].astype(jnp.int32)


def normal_values(rng, shape, width, most, shards=(), kind=jnp.bfloat16):
    level = block_scale(rng, shape, shards, -0.22, 0.18) if shards else 1.0
    values = jax.random.normal(rng, shape, jnp.float32) * width * level
    return jnp.minimum(jnp.maximum(values, -most), most).astype(kind)


def setup_inputs(seed: int = 0) -> dict:
    key_of = jax.random.split(jax.random.key(seed), 6)
    return {
        "jacobians": normal_values(key_of[0], (18, SLOTS), 0.5, 3.0, ((1, 32),), jnp.float32),
        "residuals": normal_values(key_of[1], (2, SLOTS), 1.0, 6.0, ((1, 32),), jnp.float32),
        "camera_local": set_ends(ranked_ids(key_of[2], (SLOTS,), CAM_DEV, 1), jax.random.fold_in(key_of[2], 3), 0, CAM_DEV - 1).astype(jnp.int32),
        "bucket_counts": draw_bucket_counts(jax.random.fold_in(key_of[5], 71), 0),
        "camera_map": jax.random.permutation(key_of[4], CAM).astype(jnp.int32),
    }


def observation_terms(jacobs, resids):
    leading_row = jacobs[0:9]
    trailing_row = jacobs[9:18]
    gradient_terms = leading_row * resids[0:1] + trailing_row * resids[1:2]
    block_terms = leading_row[:, None] * leading_row[None, :] + trailing_row[:, None] * trailing_row[None, :]
    block_terms = block_terms.reshape((81,) + leading_row.shape[1:])
    return jnp.concatenate([gradient_terms, block_terms], axis=0)


def reference(jacobians, residuals, camera_local, bucket_counts, camera_map):
    sources = N_OBS * N_REP
    columns = N_OBS * CAP
    jac_blocks = jnp.moveaxis(jacobians.reshape(18, sources, columns), 1, 0)
    res_blocks = jnp.moveaxis(residuals.reshape(2, sources, columns), 1, 0)
    cam_blocks = camera_local.reshape(sources, columns)
    position = jnp.arange(columns, dtype=jnp.int32)
    target = position // CAP
    within = position % CAP

    def accumulate(summed, inputs):
        jac_here, res_here, cam_here, count_here = inputs
        live_mask = (within < count_here[target]).astype(jnp.float32)
        obs_terms = observation_terms(jac_here * live_mask, res_here * live_mask)
        segment = (target * CAM_DEV + cam_here).astype(jnp.int32)
        return summed + jax.ops.segment_sum(obs_terms.T, segment, num_segments=CAM), None

    summed, unused = lax.scan(accumulate, jnp.zeros((CAM, 90), jnp.float32), (jac_blocks, res_blocks, cam_blocks, bucket_counts))
    slot_gradient = summed[:, :9].T
    camera_blocks = summed[:, 9:].T
    gradient = jnp.zeros((9, CAM), jnp.float32).at[:, camera_map].set(slot_gradient)
    return gradient, camera_blocks
```

```python
import functools

import jax
import jax.numpy as jnp
from jax import lax
from jax.experimental import pallas as pl
from jax.experimental.pallas import tpu as pltpu
from jax.sharding import PartitionSpec as P

CAM_DEV = 1024
MESH = pl.DeviceIdType.MESH
F32 = jnp.float32
BF16 = jnp.bfloat16
VMEM = pltpu.VMEM
ROWS = 64
GRAD = 48
LOW = 256


def vspec():
    return pl.BlockSpec(memory_space=VMEM)


def split(value):
    high = value.astype(BF16).astype(F32)
    return high, value - high


def pack_kernel(counts, jac, res, ids, out):
    buckets = counts.shape[1]
    cap = jac.shape[1] // buckets
    out[0:18, :] = jac[...]
    out[18:20, :] = res[...]
    place = lax.broadcasted_iota(jnp.int32, (1, cap), 1)
    for d in range(buckets):
        lanes = slice(d * cap, (d + 1) * cap)
        out[20:21, lanes] = jnp.where(place < counts[0, d], ids[:, lanes], -1).astype(F32)
    out[21:24, :] = jnp.zeros((3, jac.shape[1]), F32)


def exchange_kernel(n, packed, moved, own_sem, send_sem, recv_sem):
    me = lax.axis_index("obs")
    cap = moved.shape[2]
    barrier = pltpu.get_barrier_semaphore()
    for i in range(1, n):
        pl.semaphore_signal(barrier, inc=1, device_id={"obs": lax.rem(me + i, n)}, device_id_type=MESH)
    own = pltpu.make_async_copy(
        packed.at[:, pl.ds(pl.multiple_of(me * cap, cap), cap)], moved.at[me], own_sem
    )
    own.start()
    pl.semaphore_wait(barrier, n - 1)
    copies = []
    for i in range(1, n):
        peer = lax.rem(me + i, n)
        copy = pltpu.make_async_remote_copy(
            src_ref=packed.at[:, pl.ds(pl.multiple_of(peer * cap, cap), cap)],
            dst_ref=moved.at[me],
            send_sem=send_sem.at[i],
            recv_sem=recv_sem.at[i],
            device_id={"obs": peer},
            device_id_type=MESH,
        )
        copy.start()
        copies.append(copy)
    own.wait()
    for copy in copies:
        copy.wait()


def add_block(block, terms, acc):
    cap = block.shape[1]
    lead, trail, res = block[0:9], block[9:18], block[18:20]
    ids = block[20:21].astype(jnp.int32)
    at = 0
    for k in range(9):
        terms[at : at + 9 - k, :] = lead[k : k + 1] * lead[k:9] + trail[k : k + 1] * trail[k:9]
        at += 9 - k
    terms[GRAD : GRAD + 9, :] = lead * res[0:1] + trail * res[1:2]
    high, low = split(terms[...])
    both = jnp.concatenate([high, low], axis=0).astype(BF16)
    rows = lax.broadcasted_iota(jnp.int32, (CAM_DEV, cap), 0)
    one_hot = jnp.where(ids == rows, 1.0, 0.0).astype(BF16)
    added = lax.dot_general(both, one_hot, (((1,), (1,)), ((), ())), preferred_element_type=F32)
    acc[...] += added[:ROWS] + added[ROWS:]


def sums_kernel(moved, acc, terms):
    acc[...] = jnp.zeros_like(acc)
    terms[...] = jnp.zeros_like(terms)

    def body(s, carry):
        add_block(moved[s], terms, acc)
        return carry

    lax.fori_loop(0, moved.shape[0], body, 0)


def reduce_kernel(n, m, part, blocks, grads, landed, total, mine, a_send, a_recv, b_send, b_recv, g_send, g_recv, c_send, c_recv):
    me, rep = lax.axis_index("obs"), lax.axis_index("rep")
    width = total.shape[1]
    barrier = pltpu.get_barrier_semaphore()
    for i in range(1, m):
        pl.semaphore_signal(barrier, inc=1, device_id={"rep": lax.rem(rep + i, m)}, device_id_type=MESH)
    for i in range(1, n):
        pl.semaphore_signal(barrier, inc=1, device_id={"obs": lax.rem(me + i, n)}, device_id_type=MESH)
    pl.semaphore_wait(barrier, n + m - 2)

    def send(src, dst, s, r, axis, peer):
        copy = pltpu.make_async_remote_copy(
            src_ref=src, dst_ref=dst, send_sem=s, recv_sem=r, device_id={axis: peer}, device_id_type=MESH
        )
        copy.start()
        return copy

    first = []
    for i in range(1, m):
        peer = lax.rem(rep + i, m)
        lanes = pl.ds(pl.multiple_of(peer * width, width), width)
        first.append(send(part.at[:, lanes], landed.at[i], a_send.at[i], a_recv.at[i], "rep", peer))
    own = part[:, pl.ds(pl.multiple_of(rep * width, width), width)]
    for copy in first:
        copy.wait()
    for i in range(1, m):
        own = own + landed[i]
    total[...] = own[:GRAD]
    mine[...] = own[GRAD : GRAD + 9]
    grads[rep, me] = own[GRAD : GRAD + 9]
    blocks[rep] = own[:GRAD]
    around, sent = [], []
    for i in range(1, n):
        peer = lax.rem(me + i, n)
        around.append(
            send(mine, grads.at[rep, me], g_send.at[i], g_recv.at[i], "obs", peer)
        )
    for j in range(1, m):
        peer = lax.rem(rep + j, m)
        sent.append(
            send(mine, grads.at[rep, me], c_send.at[j, 0], c_recv.at[j, 0], "rep", peer)
        )
        sent.append(send(total, blocks.at[rep], b_send.at[j], b_recv.at[j], "rep", peer))
    for i in range(1, n):
        around[i - 1].wait_recv()
        source = lax.rem(me - i + n, n)
        for j in range(1, m):
            peer = lax.rem(rep + j, m)
            sent.append(
                send(grads.at[rep, source], grads.at[rep, source], c_send.at[j, i], c_recv.at[j, i], "rep", peer)
            )
    for copy in around:
        copy.wait_send()
    for copy in sent:
        copy.wait()


def finish_kernel(blocks, grads, cmap, gradient, out, acc):
    m, n, _, width = grads.shape
    span = m * width
    cams = n * span
    highs = cams // LOW
    at = 0
    for k in range(9):
        for l in range(k, 9):
            for r in range(m):
                row = blocks[r, at : at + 1, :]
                lanes = slice(r * width, (r + 1) * width)
                out[k * 9 + l : k * 9 + l + 1, lanes] = row
                if l != k:
                    out[l * 9 + k : l * 9 + k + 1, lanes] = row
            at += 1
    acc[...] = jnp.zeros_like(acc)

    def body(o, carry):
        slots = jnp.concatenate([grads[r, o] for r in range(m)], axis=1)
        ids = cmap[:, pl.ds(pl.multiple_of(o * span, span), span)]
        up, down = ids // LOW, lax.rem(ids, LOW)
        one_hot = jnp.where(down == lax.broadcasted_iota(jnp.int32, (LOW, span), 0), 1.0, 0.0).astype(BF16)
        high, low = split(slots)
        top = jnp.concatenate([high[0:8], low[0:8]], axis=0)
        up16 = jnp.broadcast_to(up, (16, span))
        dims = (((1,), (1,)), ((), ()))
        group = 16

        def tiles(g, carry):
            lhs = jnp.concatenate(
                [jnp.where(up16 == g * group + h, top, 0.0).astype(BF16) for h in range(group)], axis=0
            )
            where = pl.ds(pl.multiple_of(g * group * 16, group * 16), group * 16)
            acc[where, :] += lax.dot_general(lhs, one_hot, dims, preferred_element_type=F32)
            return carry

        lax.fori_loop(0, highs // group, tiles, 0)
        mask = up == lax.broadcasted_iota(jnp.int32, (highs, span), 0)
        last = jnp.concatenate([jnp.where(mask, high[8:9], 0.0), jnp.where(mask, low[8:9], 0.0)], axis=0).astype(BF16)
        acc[highs * 16 :, :] += lax.dot_general(last, one_hot, dims, preferred_element_type=F32)
        return carry

    lax.fori_loop(0, n, body, 0)
    for h in range(highs):
        lanes = slice(h * LOW, (h + 1) * LOW)
        gradient[0:8, lanes] = acc[h * 16 : h * 16 + 8, :] + acc[h * 16 + 8 : h * 16 + 16, :]
        ninth = highs * 16 + h
        gradient[8:9, lanes] = acc[ninth : ninth + 1, :] + acc[ninth + highs : ninth + highs + 1, :]


def local(jacobians, residuals, camera_local, bucket_counts, camera_map):
    n, m = lax.axis_size("obs"), lax.axis_size("rep")
    slots = jacobians.shape[1]
    cap = slots // n
    cams = camera_map.shape[0]
    width = CAM_DEV // m
    highs = cams // LOW
    limit = 60 * 1024 * 1024
    params = pltpu.CompilerParams(vmem_limit_bytes=limit)
    packed = pl.pallas_call(
        pack_kernel,
        out_shape=jax.ShapeDtypeStruct((24, slots), F32),
        in_specs=[pl.BlockSpec(memory_space=pltpu.SMEM)] + [vspec()] * 3,
        out_specs=vspec(),
        compiler_params=params,
    )(bucket_counts, jacobians, residuals, camera_local.reshape(1, slots))
    moved = pl.pallas_call(
        functools.partial(exchange_kernel, n),
        out_shape=jax.ShapeDtypeStruct((n, 24, cap), F32),
        in_specs=[vspec()],
        out_specs=vspec(),
        scratch_shapes=[
            pltpu.SemaphoreType.DMA,
            pltpu.SemaphoreType.DMA((n,)),
            pltpu.SemaphoreType.DMA((n,)),
        ],
        compiler_params=pltpu.CompilerParams(collective_id=0, has_side_effects=True, vmem_limit_bytes=limit),
    )(packed)
    part = pl.pallas_call(
        sums_kernel,
        out_shape=jax.ShapeDtypeStruct((ROWS, CAM_DEV), F32),
        in_specs=[vspec()],
        out_specs=vspec(),
        scratch_shapes=[VMEM((ROWS, cap), F32)],
        compiler_params=params,
    )(moved)
    dma = pltpu.SemaphoreType.DMA
    blocks, grads = pl.pallas_call(
        functools.partial(reduce_kernel, n, m),
        out_shape=(jax.ShapeDtypeStruct((m, GRAD, width), F32), jax.ShapeDtypeStruct((m, n, 9, width), F32)),
        in_specs=[vspec()],
        out_specs=(vspec(), vspec()),
        scratch_shapes=[
            VMEM((m, ROWS, width), F32),
            VMEM((GRAD, width), F32),
            VMEM((9, width), F32),
            dma((m,)),
            dma((m,)),
            dma((m,)),
            dma((m,)),
            dma((n,)),
            dma((n,)),
            dma((m, n)),
            dma((m, n)),
        ],
        compiler_params=pltpu.CompilerParams(collective_id=1, has_side_effects=True, vmem_limit_bytes=limit),
    )(part)
    gradient, out = pl.pallas_call(
        finish_kernel,
        out_shape=(jax.ShapeDtypeStruct((9, cams), F32), jax.ShapeDtypeStruct((81, CAM_DEV), F32)),
        in_specs=[vspec()] * 3,
        out_specs=(vspec(), vspec()),
        scratch_shapes=[VMEM((highs * 18, LOW), F32)],
        compiler_params=params,
    )(blocks, grads, camera_map.reshape(1, cams))
    return (gradient, out)


def solution(mesh):
    in_specs = (
        P(None, ("obs", "rep")),
        P(None, ("obs", "rep")),
        P(("obs", "rep")),
        P(("obs", "rep"), None),
        P(),
    )
    out_specs = (P(), P(None, "obs"))
    return jax.shard_map(local, mesh=mesh, in_specs=in_specs, out_specs=out_specs, check_vma=False)
```

```python
import functools

import jax
import jax.numpy as jnp
from jax import lax
from jax.experimental import pallas as pl
from jax.experimental.pallas import tpu as pltpu
from jax.sharding import PartitionSpec as P

CAM_DEV = 1024
MESH = pl.DeviceIdType.MESH
F32 = jnp.float32
BF16 = jnp.bfloat16
VMEM = pltpu.VMEM
ROWS = 56
GRAD = 45
KEPT = 48
LOW = 256


def vspec():
    return pl.BlockSpec(memory_space=VMEM)


def split(value):
    high = value.astype(BF16).astype(F32)
    return high, value - high


def pack(counts, jac, res, ids, out):
    buckets = counts.shape[1]
    cap = jac.shape[1] // buckets
    out[0:18, :] = jac[...]
    out[18:20, :] = res[...]
    place = lax.broadcasted_iota(jnp.int32, (1, cap), 1)
    for d in range(buckets):
        lanes = slice(d * cap, (d + 1) * cap)
        out[20:21, lanes] = jnp.where(place < counts[0, d], ids[:, lanes], -1).astype(F32)
    out[21:24, :] = jnp.zeros((3, jac.shape[1]), F32)


def add_block(block, terms, acc):
    cap = block.shape[1]
    lead, trail, res = block[0:9], block[9:18], block[18:20]
    ids = block[20:21].astype(jnp.int32)
    at = 0
    for k in range(9):
        terms[at : at + 9 - k, :] = lead[k : k + 1] * lead[k:9] + trail[k : k + 1] * trail[k:9]
        at += 9 - k
    terms[GRAD : GRAD + 9, :] = lead * res[0:1] + trail * res[1:2]
    high, low = split(terms[...])
    both = jnp.concatenate([high, low], axis=0).astype(BF16)
    rows = lax.broadcasted_iota(jnp.int32, (CAM_DEV, cap), 0)
    one_hot = jnp.where(ids == rows, 1.0, 0.0).astype(BF16)
    added = lax.dot_general(both, one_hot, (((1,), (1,)), ((), ())), preferred_element_type=F32)
    acc[...] += added[:ROWS] + added[ROWS:]


def main_kernel(
    n, m, counts, jac, res, ids, blocks, grads, packed, moved, terms, part, landed, total, mine,
    x_send, x_recv, a_send, a_recv, b_send, b_recv, g_send, g_recv, c_send, c_recv,
):
    me, rep = lax.axis_index("obs"), lax.axis_index("rep")
    width = total.shape[1]
    cap = moved.shape[2]
    barrier = pltpu.get_barrier_semaphore()
    for i in range(1, n):
        pl.semaphore_signal(barrier, inc=1, device_id={"obs": lax.rem(me + i, n)}, device_id_type=MESH)
    for i in range(1, m):
        pl.semaphore_signal(barrier, inc=1, device_id={"rep": lax.rem(rep + i, m)}, device_id_type=MESH)
    pack(counts, jac, res, ids, packed)
    part[...] = jnp.zeros_like(part)
    terms[...] = jnp.zeros_like(terms)
    pl.semaphore_wait(barrier, n + m - 2)

    def lanes_of(peer):
        return pl.ds(pl.multiple_of(peer * cap, cap), cap)

    def handing(i):
        peer = lax.rem(me + i, n)
        return pltpu.make_async_remote_copy(
            src_ref=packed.at[:, lanes_of(peer)],
            dst_ref=moved.at[i],
            send_sem=x_send.at[i],
            recv_sem=x_recv.at[i],
            device_id={"obs": peer},
            device_id_type=MESH,
        )

    def start(i, carry):
        handing(i).start()
        return carry

    def take(i, carry):
        handing(i).wait_recv()
        add_block(moved[i], terms, part)
        return carry

    def drain(i, carry):
        handing(i).wait_send()
        return carry

    lax.fori_loop(1, n, start, 0)
    add_block(packed[:, lanes_of(me)], terms, part)
    lax.fori_loop(1, n, take, 0)

    def send(src, dst, s, r, axis, peer):
        copy = pltpu.make_async_remote_copy(
            src_ref=src, dst_ref=dst, send_sem=s, recv_sem=r, device_id={axis: peer}, device_id_type=MESH
        )
        copy.start()
        return copy

    first = []
    for i in range(1, m):
        peer = lax.rem(rep + i, m)
        lanes = pl.ds(pl.multiple_of(peer * width, width), width)
        first.append(send(part.at[:, lanes], landed.at[i], a_send.at[i], a_recv.at[i], "rep", peer))
    lax.fori_loop(1, n, drain, 0)
    own = part[:, pl.ds(pl.multiple_of(rep * width, width), width)]
    for copy in first:
        copy.wait()
    for i in range(1, m):
        own = own + landed[i]
    total[...] = own[:KEPT]
    mine[...] = own[GRAD : GRAD + 9]
    grads[rep, me] = own[GRAD : GRAD + 9]
    blocks[rep] = own[:KEPT]
    around, sent = [], []
    for i in range(1, n):
        peer = lax.rem(me + i, n)
        around.append(
            send(mine, grads.at[rep, me], g_send.at[i], g_recv.at[i], "obs", peer)
        )
    for j in range(1, m):
        peer = lax.rem(rep + j, m)
        sent.append(
            send(mine, grads.at[rep, me], c_send.at[j, 0], c_recv.at[j, 0], "rep", peer)
        )
        sent.append(send(total, blocks.at[rep], b_send.at[j], b_recv.at[j], "rep", peer))
    for i in range(1, n):
        around[i - 1].wait_recv()
        source = lax.rem(me - i + n, n)
        for j in range(1, m):
            peer = lax.rem(rep + j, m)
            sent.append(
                send(grads.at[rep, source], grads.at[rep, source], c_send.at[j, i], c_recv.at[j, i], "rep", peer)
            )
    for copy in around:
        copy.wait_send()
    for copy in sent:
        copy.wait()


def finish_kernel(blocks, grads, cmap, gradient, out, acc):
    m, n, _, width = grads.shape
    span = m * width
    cams = n * span
    highs = cams // LOW
    at = 0
    for k in range(9):
        for l in range(k, 9):
            for r in range(m):
                row = blocks[r, at : at + 1, :]
                lanes = slice(r * width, (r + 1) * width)
                out[k * 9 + l : k * 9 + l + 1, lanes] = row
                if l != k:
                    out[l * 9 + k : l * 9 + k + 1, lanes] = row
            at += 1
    acc[...] = jnp.zeros_like(acc)

    def body(o, carry):
        slots = jnp.concatenate([grads[r, o] for r in range(m)], axis=1)
        ids = cmap[:, pl.ds(pl.multiple_of(o * span, span), span)]
        up, down = ids // LOW, lax.rem(ids, LOW)
        one_hot = jnp.where(down == lax.broadcasted_iota(jnp.int32, (LOW, span), 0), 1.0, 0.0).astype(BF16)
        high, low = split(slots)
        top = jnp.concatenate([high[0:8], low[0:8]], axis=0)
        up16 = jnp.broadcast_to(up, (16, span))
        dims = (((1,), (1,)), ((), ()))
        group = 16

        def tiles(g, carry):
            lhs = jnp.concatenate(
                [jnp.where(up16 == g * group + h, top, 0.0).astype(BF16) for h in range(group)], axis=0
            )
            where = pl.ds(pl.multiple_of(g * group * 16, group * 16), group * 16)
            acc[where, :] += lax.dot_general(lhs, one_hot, dims, preferred_element_type=F32)
            return carry

        lax.fori_loop(0, highs // group, tiles, 0)
        mask = up == lax.broadcasted_iota(jnp.int32, (highs, span), 0)
        last = jnp.concatenate([jnp.where(mask, high[8:9], 0.0), jnp.where(mask, low[8:9], 0.0)], axis=0).astype(BF16)
        acc[highs * 16 :, :] += lax.dot_general(last, one_hot, dims, preferred_element_type=F32)
        return carry

    lax.fori_loop(0, n, body, 0)
    for h in range(highs):
        lanes = slice(h * LOW, (h + 1) * LOW)
        gradient[0:8, lanes] = acc[h * 16 : h * 16 + 8, :] + acc[h * 16 + 8 : h * 16 + 16, :]
        ninth = highs * 16 + h
        gradient[8:9, lanes] = acc[ninth : ninth + 1, :] + acc[ninth + highs : ninth + highs + 1, :]


def local(jacobians, residuals, camera_local, bucket_counts, camera_map):
    n, m = lax.axis_size("obs"), lax.axis_size("rep")
    slots = jacobians.shape[1]
    cap = slots // n
    cams = camera_map.shape[0]
    width = CAM_DEV // m
    highs = cams // LOW
    limit = 60 * 1024 * 1024
    params = pltpu.CompilerParams(vmem_limit_bytes=limit)
    dma = pltpu.SemaphoreType.DMA
    blocks, grads = pl.pallas_call(
        functools.partial(main_kernel, n, m),
        out_shape=(jax.ShapeDtypeStruct((m, KEPT, width), F32), jax.ShapeDtypeStruct((m, n, 9, width), F32)),
        in_specs=[pl.BlockSpec(memory_space=pltpu.SMEM)] + [vspec()] * 3,
        out_specs=(vspec(), vspec()),
        scratch_shapes=[
            VMEM((24, slots), F32),
            VMEM((n, 24, cap), F32),
            VMEM((ROWS, cap), F32),
            VMEM((ROWS, CAM_DEV), F32),
            VMEM((m, ROWS, width), F32),
            VMEM((KEPT, width), F32),
            VMEM((9, width), F32),
            dma((n,)),
            dma((n,)),
            dma((m,)),
            dma((m,)),
            dma((m,)),
            dma((m,)),
            dma((n,)),
            dma((n,)),
            dma((m, n)),
            dma((m, n)),
        ],
        compiler_params=pltpu.CompilerParams(collective_id=0, has_side_effects=True, vmem_limit_bytes=limit),
    )(bucket_counts, jacobians, residuals, camera_local.reshape(1, slots))
    gradient, out = pl.pallas_call(
        finish_kernel,
        out_shape=(jax.ShapeDtypeStruct((9, cams), F32), jax.ShapeDtypeStruct((81, CAM_DEV), F32)),
        in_specs=[vspec()] * 3,
        out_specs=(vspec(), vspec()),
        scratch_shapes=[VMEM((highs * 18, LOW), F32)],
        compiler_params=params,
    )(blocks, grads, camera_map.reshape(1, cams))
    return (gradient, out)


def solution(mesh):
    in_specs = (
        P(None, ("obs", "rep")),
        P(None, ("obs", "rep")),
        P(("obs", "rep")),
        P(("obs", "rep"), None),
        P(),
    )
    out_specs = (P(), P(None, "obs"))
    return jax.shard_map(local, mesh=mesh, in_specs=in_specs, out_specs=out_specs, check_vma=False)
```

```python
import functools

import jax
import jax.numpy as jnp
from jax import lax
from jax.experimental import pallas as pl
from jax.experimental.pallas import tpu as pltpu
from jax.sharding import PartitionSpec as P

CAM_DEV = 1024
MESH = pl.DeviceIdType.MESH
F32 = jnp.float32
BF16 = jnp.bfloat16
VMEM = pltpu.VMEM
ROWS = 56
GRAD = 45
KEPT = 48
LOW = 256


def vspec():
    return pl.BlockSpec(memory_space=VMEM)


def split(value):
    high = value.astype(BF16).astype(F32)
    return high, value - high


def pack(counts, jac, res, ids, out):
    buckets = counts.shape[1]
    cap = jac.shape[1] // buckets
    out[0:18, :] = jac[...]
    out[18:20, :] = res[...]
    place = lax.broadcasted_iota(jnp.int32, (1, cap), 1)
    for d in range(buckets):
        lanes = slice(d * cap, (d + 1) * cap)
        out[20:21, lanes] = jnp.where(place < counts[0, d], ids[:, lanes], -1).astype(F32)
    out[21:24, :] = jnp.zeros((3, jac.shape[1]), F32)


def one_hot_of(low, wide):
    shape = (wide, low.shape[1])
    rows = lax.broadcasted_iota(jnp.int32, shape, 0).astype(F32).astype(BF16)
    there = jnp.broadcast_to(low.astype(F32), shape).astype(BF16)
    return jnp.where(there == rows, jnp.ones(shape, BF16), jnp.zeros(shape, BF16))


def add_block(block, terms, acc):
    cap = block.shape[1]
    lead, trail, res = block[0:9], block[9:18], block[18:20]
    ids = block[20:21].astype(jnp.int32)
    at = 0
    for k in range(9):
        terms[at : at + 9 - k, :] = lead[k : k + 1] * lead[k:9] + trail[k : k + 1] * trail[k:9]
        at += 9 - k
    terms[GRAD : GRAD + 9, :] = lead * res[0:1] + trail * res[1:2]
    high, low = split(terms[...])
    both = jnp.concatenate([high, low], axis=0).astype(BF16)
    pieces, _, width = acc.shape
    up = jnp.where(ids < 0, -1, ids // width)
    down = ids - up * width
    one_hot = one_hot_of(down, width)
    up = jnp.broadcast_to(up.astype(F32), both.shape).astype(BF16)
    zero = jnp.zeros_like(both)
    lhs = jnp.concatenate([jnp.where(up == jnp.asarray(h, BF16), both, zero) for h in range(pieces)], axis=0)
    added = lax.dot_general(lhs, one_hot, (((1,), (1,)), ((), ())), preferred_element_type=F32)
    for h in range(pieces):
        at = h * 2 * ROWS
        acc[h] += added[at : at + ROWS] + added[at + ROWS : at + 2 * ROWS]


def main_kernel(
    n, m, counts, jac, res, ids, blocks, grads, packed, moved, terms, part, landed, total, mine,
    x_send, x_recv, a_send, a_recv, b_send, b_recv, g_send, g_recv, c_send, c_recv,
):
    me, rep = lax.axis_index("obs"), lax.axis_index("rep")
    width = total.shape[1]
    cap = moved.shape[2]
    barrier = pltpu.get_barrier_semaphore()
    for i in range(1, n):
        pl.semaphore_signal(barrier, inc=1, device_id={"obs": lax.rem(me + i, n)}, device_id_type=MESH)
    for i in range(1, m):
        pl.semaphore_signal(barrier, inc=1, device_id={"rep": lax.rem(rep + i, m)}, device_id_type=MESH)
    pack(counts, jac, res, ids, packed)
    part[...] = jnp.zeros_like(part)
    terms[...] = jnp.zeros_like(terms)
    pl.semaphore_wait(barrier, n + m - 2)

    def lanes_of(peer):
        return pl.ds(pl.multiple_of(peer * cap, cap), cap)

    def handing(i):
        peer = lax.rem(me + i, n)
        return pltpu.make_async_remote_copy(
            src_ref=packed.at[:, lanes_of(peer)],
            dst_ref=moved.at[i],
            send_sem=x_send.at[i],
            recv_sem=x_recv.at[i],
            device_id={"obs": peer},
            device_id_type=MESH,
        )

    def start(i, carry):
        handing(i).start()
        return carry

    def take(i, carry):
        handing(i).wait_recv()
        add_block(moved[i], terms, part)
        return carry

    def drain(i, carry):
        handing(i).wait_send()
        return carry

    lax.fori_loop(1, n, start, 0)
    add_block(packed[:, lanes_of(me)], terms, part)
    lax.fori_loop(1, n, take, 0)

    def send(src, dst, s, r, axis, peer):
        copy = pltpu.make_async_remote_copy(
            src_ref=src, dst_ref=dst, send_sem=s, recv_sem=r, device_id={axis: peer}, device_id_type=MESH
        )
        copy.start()
        return copy

    first = []
    for i in range(1, m):
        peer = lax.rem(rep + i, m)
        first.append(send(part.at[peer], landed.at[i], a_send.at[i], a_recv.at[i], "rep", peer))
    lax.fori_loop(1, n, drain, 0)
    own = part[rep]
    for copy in first:
        copy.wait()
    for i in range(1, m):
        own = own + landed[i]
    total[...] = own[:KEPT]
    mine[...] = own[GRAD : GRAD + 9]
    grads[rep, me] = own[GRAD : GRAD + 9]
    blocks[rep] = own[:KEPT]
    around, sent = [], []
    for i in range(1, n):
        peer = lax.rem(me + i, n)
        around.append(
            send(mine, grads.at[rep, me], g_send.at[i], g_recv.at[i], "obs", peer)
        )
    for j in range(1, m):
        peer = lax.rem(rep + j, m)
        sent.append(
            send(mine, grads.at[rep, me], c_send.at[j, 0], c_recv.at[j, 0], "rep", peer)
        )
        sent.append(send(total, blocks.at[rep], b_send.at[j], b_recv.at[j], "rep", peer))
    for i in range(1, n):
        around[i - 1].wait_recv()
        source = lax.rem(me - i + n, n)
        for j in range(1, m):
            peer = lax.rem(rep + j, m)
            sent.append(
                send(grads.at[rep, source], grads.at[rep, source], c_send.at[j, i], c_recv.at[j, i], "rep", peer)
            )
    for copy in around:
        copy.wait_send()
    for copy in sent:
        copy.wait()


def finish_kernel(blocks, grads, cmap, gradient, out, acc):
    m, n, _, width = grads.shape
    span = m * width
    cams = n * span
    highs = cams // LOW
    at = 0
    for k in range(9):
        for l in range(k, 9):
            for r in range(m):
                row = blocks[r, at : at + 1, :]
                lanes = slice(r * width, (r + 1) * width)
                out[k * 9 + l : k * 9 + l + 1, lanes] = row
                if l != k:
                    out[l * 9 + k : l * 9 + k + 1, lanes] = row
            at += 1
    acc[...] = jnp.zeros_like(acc)

    def body(o, carry):
        slots = jnp.concatenate([grads[r, o] for r in range(m)], axis=1)
        ids = cmap[:, pl.ds(pl.multiple_of(o * span, span), span)]
        up, down = ids // LOW, lax.rem(ids, LOW)
        one_hot = one_hot_of(down, LOW)
        high, low = split(slots)
        top = jnp.concatenate([high[0:8], low[0:8]], axis=0).astype(BF16)
        up16 = jnp.broadcast_to(up.astype(F32), (16, span)).astype(BF16)
        none = jnp.zeros_like(top)
        mask = up == lax.broadcasted_iota(jnp.int32, (highs, span), 0)
        last = jnp.concatenate([jnp.where(mask, high[8:9], 0.0), jnp.where(mask, low[8:9], 0.0)], axis=0).astype(BF16)
        dims = (((1,), (1,)), ((), ()))
        group = min(highs, 32)

        def tiles(start):
            return [
                jnp.where(up16 == jnp.asarray(start + h, F32).astype(BF16), top, none) for h in range(group)
            ]

        if group == highs:
            lhs = jnp.concatenate(tiles(0) + [last], axis=0)
            acc[...] += lax.dot_general(lhs, one_hot, dims, preferred_element_type=F32)
            return carry

        def some(g, carry):
            lhs = jnp.concatenate(tiles(g * group), axis=0)
            where = pl.ds(pl.multiple_of(g * group * 16, group * 16), group * 16)
            acc[where, :] += lax.dot_general(lhs, one_hot, dims, preferred_element_type=F32)
            return carry

        lax.fori_loop(0, highs // group, some, 0)
        acc[highs * 16 :, :] += lax.dot_general(last, one_hot, dims, preferred_element_type=F32)
        return carry

    lax.fori_loop(0, n, body, 0)
    for h in range(highs):
        lanes = slice(h * LOW, (h + 1) * LOW)
        gradient[0:8, lanes] = acc[h * 16 : h * 16 + 8, :] + acc[h * 16 + 8 : h * 16 + 16, :]
        ninth = highs * 16 + h
        gradient[8:9, lanes] = acc[ninth : ninth + 1, :] + acc[ninth + highs : ninth + highs + 1, :]


def local(jacobians, residuals, camera_local, bucket_counts, camera_map):
    n, m = lax.axis_size("obs"), lax.axis_size("rep")
    slots = jacobians.shape[1]
    cap = slots // n
    cams = camera_map.shape[0]
    width = CAM_DEV // m
    highs = cams // LOW
    limit = 60 * 1024 * 1024
    params = pltpu.CompilerParams(vmem_limit_bytes=limit)
    dma = pltpu.SemaphoreType.DMA
    blocks, grads = pl.pallas_call(
        functools.partial(main_kernel, n, m),
        out_shape=(jax.ShapeDtypeStruct((m, KEPT, width), F32), jax.ShapeDtypeStruct((m, n, 9, width), F32)),
        in_specs=[pl.BlockSpec(memory_space=pltpu.SMEM)] + [vspec()] * 3,
        out_specs=(vspec(), vspec()),
        scratch_shapes=[
            VMEM((24, slots), F32),
            VMEM((n, 24, cap), F32),
            VMEM((ROWS, cap), F32),
            VMEM((m, ROWS, width), F32),
            VMEM((m, ROWS, width), F32),
            VMEM((KEPT, width), F32),
            VMEM((9, width), F32),
            dma((n,)),
            dma((n,)),
            dma((m,)),
            dma((m,)),
            dma((m,)),
            dma((m,)),
            dma((n,)),
            dma((n,)),
            dma((m, n)),
            dma((m, n)),
        ],
        compiler_params=pltpu.CompilerParams(collective_id=0, has_side_effects=True, vmem_limit_bytes=limit),
    )(bucket_counts, jacobians, residuals, camera_local.reshape(1, slots))
    gradient, out = pl.pallas_call(
        finish_kernel,
        out_shape=(jax.ShapeDtypeStruct((9, cams), F32), jax.ShapeDtypeStruct((81, CAM_DEV), F32)),
        in_specs=[vspec()] * 3,
        out_specs=(vspec(), vspec()),
        scratch_shapes=[VMEM((highs * 18, LOW), F32)],
        compiler_params=params,
    )(blocks, grads, camera_map.reshape(1, cams))
    return (gradient, out)


def solution(mesh):
    in_specs = (
        P(None, ("obs", "rep")),
        P(None, ("obs", "rep")),
        P(("obs", "rep")),
        P(("obs", "rep"), None),
        P(),
    )
    out_specs = (P(), P(None, "obs"))
    return jax.shard_map(local, mesh=mesh, in_specs=in_specs, out_specs=out_specs, check_vma=False)
```

```python
import functools

import jax
import jax.numpy as jnp
from jax import lax
from jax.experimental import pallas as pl
from jax.experimental.pallas import tpu as pltpu
from jax.sharding import PartitionSpec as P

CAM_DEV = 1024
MESH = pl.DeviceIdType.MESH
F32 = jnp.float32
BF16 = jnp.bfloat16
VMEM = pltpu.VMEM
ROWS = 56
GRAD = 45
KEPT = 48
LOW = 256


def vspec():
    return pl.BlockSpec(memory_space=VMEM)


def split(value):
    high = value.astype(BF16).astype(F32)
    return high, value - high


def pack(counts, jac, res, ids, out):
    buckets = counts.shape[1]
    cap = jac.shape[1] // buckets
    out[0:18, :] = jac[...]
    out[18:20, :] = res[...]
    place = lax.broadcasted_iota(jnp.int32, (1, cap), 1)
    for d in range(buckets):
        lanes = slice(d * cap, (d + 1) * cap)
        out[20:21, lanes] = jnp.where(place < counts[0, d], ids[:, lanes], -1).astype(F32)


def one_hot_of(low, wide):
    shape = (wide, low.shape[1])
    rows = lax.broadcasted_iota(jnp.int32, shape, 0).astype(F32).astype(BF16)
    there = jnp.broadcast_to(low.astype(F32), shape).astype(BF16)
    return jnp.where(there == rows, jnp.ones(shape, BF16), jnp.zeros(shape, BF16))


def add_block(block, terms, acc):
    cap = block.shape[1]
    lead, trail, res = block[0:9], block[9:18], block[18:20]
    ids = block[20:21].astype(jnp.int32)
    at = 0
    for k in range(9):
        terms[at : at + 9 - k, :] = lead[k : k + 1] * lead[k:9] + trail[k : k + 1] * trail[k:9]
        at += 9 - k
    terms[GRAD : GRAD + 9, :] = lead * res[0:1] + trail * res[1:2]
    high, low = split(terms[...])
    both = jnp.concatenate([high, low], axis=0).astype(BF16)
    pieces, _, width = acc.shape
    up = jnp.where(ids < 0, -1, ids // width)
    down = ids - up * width
    one_hot = one_hot_of(down, width)
    up = jnp.broadcast_to(up.astype(F32), both.shape).astype(BF16)
    zero = jnp.zeros_like(both)
    lhs = jnp.concatenate([jnp.where(up == jnp.asarray(h, BF16), both, zero) for h in range(pieces)], axis=0)
    added = lax.dot_general(lhs, one_hot, (((1,), (1,)), ((), ())), preferred_element_type=F32)
    for h in range(pieces):
        at = h * 2 * ROWS
        acc[h] += added[at : at + ROWS] + added[at + ROWS : at + 2 * ROWS]


def expand(blocks, out):
    m, _, width = blocks.shape
    at = 0
    for k in range(9):
        for l in range(k, 9):
            for r in range(m):
                row = blocks[r, at : at + 1, :]
                lanes = slice(r * width, (r + 1) * width)
                out[k * 9 + l : k * 9 + l + 1, lanes] = row
                if l != k:
                    out[l * 9 + k : l * 9 + k + 1, lanes] = row
            at += 1


def place_chunk(o, grads, cmap, ready, acc):
    m, n, _, width = grads.shape
    span = m * width
    highs = n * span // LOW
    slots = jnp.concatenate([grads[r, o] for r in range(m)], axis=1)
    ids = cmap[:, pl.ds(pl.multiple_of(o * span, span), span)]
    up = ids // LOW
    one_hot = one_hot_of(lax.rem(ids, LOW), LOW) if ready is None else ready[o]
    high, low = split(slots)
    top = jnp.concatenate([high[0:8], low[0:8]], axis=0).astype(BF16)
    up16 = jnp.broadcast_to(up.astype(F32), (16, span)).astype(BF16)
    none = jnp.zeros_like(top)
    mask = up == lax.broadcasted_iota(jnp.int32, (highs, span), 0)
    last = jnp.concatenate([jnp.where(mask, high[8:9], 0.0), jnp.where(mask, low[8:9], 0.0)], axis=0).astype(BF16)
    dims = (((1,), (1,)), ((), ()))
    group = min(highs, 32)

    def tiles(start):
        return [jnp.where(up16 == jnp.asarray(start + h, F32).astype(BF16), top, none) for h in range(group)]

    if group == highs:
        lhs = jnp.concatenate(tiles(0) + [last], axis=0)
        acc[...] += lax.dot_general(lhs, one_hot, dims, preferred_element_type=F32)
        return

    def some(g, carry):
        lhs = jnp.concatenate(tiles(g * group), axis=0)
        where = pl.ds(pl.multiple_of(g * group * 16, group * 16), group * 16)
        acc[where, :] += lax.dot_general(lhs, one_hot, dims, preferred_element_type=F32)
        return carry

    lax.fori_loop(0, highs // group, some, 0)
    acc[highs * 16 :, :] += lax.dot_general(last, one_hot, dims, preferred_element_type=F32)


def lay_out(acc, gradient):
    highs = gradient.shape[1] // LOW
    for h in range(highs):
        lanes = slice(h * LOW, (h + 1) * LOW)
        gradient[0:8, lanes] = acc[h * 16 : h * 16 + 8, :] + acc[h * 16 + 8 : h * 16 + 16, :]
        ninth = highs * 16 + h
        gradient[8:9, lanes] = acc[ninth : ninth + 1, :] + acc[ninth + highs : ninth + highs + 1, :]


def main_kernel(
    n, m, counts, jac, res, ids, cmap, gradient, out, blocks, grads, ready, spread, packed, moved, terms, part, landed, total, mine,
    x_send, x_recv, a_send, a_recv, b_send, b_recv, g_send, g_recv, c_send, c_recv,
):
    me, rep = lax.axis_index("obs"), lax.axis_index("rep")
    width = total.shape[1]
    cap = moved.shape[2]
    barrier = pltpu.get_barrier_semaphore()
    for i in range(1, n):
        pl.semaphore_signal(barrier, inc=1, device_id={"obs": lax.rem(me + i, n)}, device_id_type=MESH)
    for i in range(1, m):
        pl.semaphore_signal(barrier, inc=1, device_id={"rep": lax.rem(rep + i, m)}, device_id_type=MESH)
    pack(counts, jac, res, ids, packed)
    part[...] = jnp.zeros_like(part)
    terms[...] = jnp.zeros_like(terms)
    pl.semaphore_wait(barrier, n + m - 2)

    def lanes_of(peer):
        return pl.ds(pl.multiple_of(peer * cap, cap), cap)

    def handing(i):
        peer = lax.rem(me + i, n)
        return pltpu.make_async_remote_copy(
            src_ref=packed.at[:, lanes_of(peer)],
            dst_ref=moved.at[i],
            send_sem=x_send.at[i],
            recv_sem=x_recv.at[i],
            device_id={"obs": peer},
            device_id_type=MESH,
        )

    def start(i, carry):
        handing(i).start()
        return carry

    def take(i, carry):
        handing(i).wait_recv()
        add_block(moved[i], terms, part)
        return carry

    def drain(i, carry):
        handing(i).wait_send()
        return carry

    lax.fori_loop(1, n, start, 0)
    add_block(packed[:, lanes_of(me)], terms, part)
    early = ready.shape[0] == n
    span = m * width

    def prepare(o, carry):
        ids_here = cmap[:, pl.ds(pl.multiple_of(o * span, span), span)]
        ready[o] = one_hot_of(lax.rem(ids_here, LOW), LOW)
        return carry

    if early:
        lax.fori_loop(0, n, prepare, 0)
    spread[...] = jnp.zeros_like(spread)
    lax.fori_loop(1, n, take, 0)

    def send(src, dst, s, r, axis, peer):
        copy = pltpu.make_async_remote_copy(
            src_ref=src, dst_ref=dst, send_sem=s, recv_sem=r, device_id={axis: peer}, device_id_type=MESH
        )
        copy.start()
        return copy

    first = []
    for i in range(1, m):
        peer = lax.rem(rep + i, m)
        first.append(send(part.at[peer], landed.at[i], a_send.at[i], a_recv.at[i], "rep", peer))
    lax.fori_loop(1, n, drain, 0)
    own = part[rep]
    for copy in first:
        copy.wait()
    for i in range(1, m):
        own = own + landed[i]
    total[...] = own[:KEPT]
    mine[...] = own[GRAD : GRAD + 9]
    grads[rep, me] = own[GRAD : GRAD + 9]
    blocks[rep] = own[:KEPT]
    around, wide, across = [], [], {}
    for i in range(1, n):
        peer = lax.rem(me + i, n)
        around.append(send(mine, grads.at[rep, me], g_send.at[i], g_recv.at[i], "obs", peer))
    for j in range(1, m):
        peer = lax.rem(rep + j, m)
        across[j, 0] = send(mine, grads.at[rep, me], c_send.at[j, 0], c_recv.at[j, 0], "rep", peer)
        wide.append(send(total, blocks.at[rep], b_send.at[j], b_recv.at[j], "rep", peer))
    for i in range(1, n):
        around[i - 1].wait_recv()
        source = lax.rem(me - i + n, n)
        for j in range(1, m):
            peer = lax.rem(rep + j, m)
            piece = grads.at[rep, source]
            across[j, i] = send(piece, piece, c_send.at[j, i], c_recv.at[j, i], "rep", peer)
    for copy in wide:
        copy.wait()
    expand(blocks, out)

    def settle(i, carry):
        source = lax.rem(me - i + n, n)
        for j in range(1, m):
            piece = grads.at[rep, source]
            pltpu.make_async_remote_copy(
                src_ref=piece, dst_ref=piece, send_sem=c_send.at[j, i], recv_sem=c_recv.at[j, i],
                device_id={"rep": lax.rem(rep + j, m)}, device_id_type=MESH,
            ).wait_recv()
        place_chunk(source, grads, cmap, ready if early else None, spread)
        return carry

    lax.fori_loop(0, n, settle, 0)
    lay_out(spread, gradient)
    for copy in around:
        copy.wait_send()
    for copy in across.values():
        copy.wait_send()


def local(jacobians, residuals, camera_local, bucket_counts, camera_map):
    n, m = lax.axis_size("obs"), lax.axis_size("rep")
    slots = jacobians.shape[1]
    cap = slots // n
    cams = camera_map.shape[0]
    width = CAM_DEV // m
    highs = cams // LOW
    limit = 60 * 1024 * 1024
    dma = pltpu.SemaphoreType.DMA
    early = n if n * LOW * CAM_DEV * 2 <= 8 * 1024 * 1024 else 1
    gradient, out = pl.pallas_call(
        functools.partial(main_kernel, n, m),
        out_shape=(jax.ShapeDtypeStruct((9, cams), F32), jax.ShapeDtypeStruct((81, CAM_DEV), F32)),
        in_specs=[pl.BlockSpec(memory_space=pltpu.SMEM)] + [vspec()] * 4,
        out_specs=(vspec(), vspec()),
        scratch_shapes=[
            VMEM((m, KEPT, width), F32),
            VMEM((m, n, 9, width), F32),
            VMEM((early, LOW, CAM_DEV), BF16),
            VMEM((highs * 18, LOW), F32),
            VMEM((21, slots), F32),
            VMEM((n, 21, cap), F32),
            VMEM((ROWS, cap), F32),
            VMEM((m, ROWS, width), F32),
            VMEM((m, ROWS, width), F32),
            VMEM((KEPT, width), F32),
            VMEM((9, width), F32),
            dma((n,)),
            dma((n,)),
            dma((m,)),
            dma((m,)),
            dma((m,)),
            dma((m,)),
            dma((n,)),
            dma((n,)),
            dma((m, n)),
            dma((m, n)),
        ],
        compiler_params=pltpu.CompilerParams(collective_id=0, has_side_effects=True, vmem_limit_bytes=limit),
    )(bucket_counts, jacobians, residuals, camera_local.reshape(1, slots), camera_map.reshape(1, cams))
    return (gradient, out)


def solution(mesh):
    in_specs = (
        P(None, ("obs", "rep")),
        P(None, ("obs", "rep")),
        P(("obs", "rep")),
        P(("obs", "rep"), None),
        P(),
    )
    out_specs = (P(), P(None, "obs"))
    return jax.shard_map(local, mesh=mesh, in_specs=in_specs, out_specs=out_specs, check_vma=False)
```

```python
import functools

import jax
import jax.numpy as jnp
from jax import lax
from jax.experimental import pallas as pl
from jax.experimental.pallas import tpu as pltpu
from jax.sharding import PartitionSpec as P

CAM_DEV = 1024
MESH = pl.DeviceIdType.MESH
F32 = jnp.float32
BF16 = jnp.bfloat16
VMEM = pltpu.VMEM
ROWS = 56
GRAD = 45
KEPT = 48
LOW = 256


def vspec():
    return pl.BlockSpec(memory_space=VMEM)


def split(value):
    high = value.astype(BF16).astype(F32)
    return high, value - high


def pack(counts, jac, res, ids, out):
    buckets = counts.shape[1]
    cap = jac.shape[1] // buckets
    out[0:18, :] = jac[...]
    out[18:20, :] = res[...]
    place = lax.broadcasted_iota(jnp.int32, (1, cap), 1)
    for d in range(buckets):
        lanes = slice(d * cap, (d + 1) * cap)
        out[20:21, lanes] = jnp.where(place < counts[0, d], ids[:, lanes], -1).astype(F32)


def one_hot_of(low, wide):
    shape = (wide, low.shape[1])
    rows = lax.broadcasted_iota(jnp.int32, shape, 0).astype(F32).astype(BF16)
    there = jnp.broadcast_to(low.astype(F32), shape).astype(BF16)
    return jnp.where(there == rows, jnp.ones(shape, BF16), jnp.zeros(shape, BF16))


def add_block(block, terms, acc):
    cap = block.shape[1]
    lead, trail, res = block[0:9], block[9:18], block[18:20]
    ids = block[20:21].astype(jnp.int32)
    at = 0
    for k in range(9):
        terms[at : at + 9 - k, :] = lead[k : k + 1] * lead[k:9] + trail[k : k + 1] * trail[k:9]
        at += 9 - k
    terms[GRAD : GRAD + 9, :] = lead * res[0:1] + trail * res[1:2]
    high, low = split(terms[...])
    both = jnp.concatenate([high, low], axis=0).astype(BF16)
    pieces, _, width = acc.shape
    up = jnp.where(ids < 0, -1, ids // width)
    down = ids - up * width
    one_hot = one_hot_of(down, width)
    up = jnp.broadcast_to(up.astype(F32), both.shape).astype(BF16)
    zero = jnp.zeros_like(both)
    lhs = jnp.concatenate([jnp.where(up == jnp.asarray(h, BF16), both, zero) for h in range(pieces)], axis=0)
    added = lax.dot_general(lhs, one_hot, (((1,), (1,)), ((), ())), preferred_element_type=F32)
    for h in range(pieces):
        at = h * 2 * ROWS
        acc[h] += added[at : at + ROWS] + added[at + ROWS : at + 2 * ROWS]


def expand(blocks, out):
    m, _, width = blocks.shape
    at = 0
    for k in range(9):
        for l in range(k, 9):
            for r in range(m):
                row = blocks[r, at : at + 1, :]
                lanes = slice(r * width, (r + 1) * width)
                out[k * 9 + l : k * 9 + l + 1, lanes] = row
                if l != k:
                    out[l * 9 + k : l * 9 + k + 1, lanes] = row
            at += 1


def place_chunk(o, grads, cmap, ready, acc):
    m, n, _, width = grads.shape
    span = m * width
    highs = n * span // LOW
    slots = jnp.concatenate([grads[r, o] for r in range(m)], axis=1)
    ids = cmap[:, pl.ds(pl.multiple_of(o * span, span), span)]
    up = ids // LOW
    one_hot = one_hot_of(lax.rem(ids, LOW), LOW) if ready is None else ready[o]
    high, low = split(slots)
    top = jnp.concatenate([high[0:8], low[0:8]], axis=0).astype(BF16)
    up16 = jnp.broadcast_to(up.astype(F32), (16, span)).astype(BF16)
    none = jnp.zeros_like(top)
    mask = up == lax.broadcasted_iota(jnp.int32, (highs, span), 0)
    last = jnp.concatenate([jnp.where(mask, high[8:9], 0.0), jnp.where(mask, low[8:9], 0.0)], axis=0).astype(BF16)
    dims = (((1,), (1,)), ((), ()))
    group = min(highs, 32)

    def tiles(start):
        return [jnp.where(up16 == jnp.asarray(start + h, F32).astype(BF16), top, none) for h in range(group)]

    if group == highs:
        lhs = jnp.concatenate(tiles(0) + [last], axis=0)
        acc[...] += lax.dot_general(lhs, one_hot, dims, preferred_element_type=F32)
        return

    def some(g, carry):
        lhs = jnp.concatenate(tiles(g * group), axis=0)
        where = pl.ds(pl.multiple_of(g * group * 16, group * 16), group * 16)
        acc[where, :] += lax.dot_general(lhs, one_hot, dims, preferred_element_type=F32)
        return carry

    lax.fori_loop(0, highs // group, some, 0)
    acc[highs * 16 :, :] += lax.dot_general(last, one_hot, dims, preferred_element_type=F32)


def lay_out(acc, gradient):
    highs = gradient.shape[1] // LOW
    for h in range(highs):
        lanes = slice(h * LOW, (h + 1) * LOW)
        gradient[0:8, lanes] = acc[h * 16 : h * 16 + 8, :] + acc[h * 16 + 8 : h * 16 + 16, :]
        ninth = highs * 16 + h
        gradient[8:9, lanes] = acc[ninth : ninth + 1, :] + acc[ninth + highs : ninth + highs + 1, :]


def main_kernel(
    n, m, counts, jac, res, ids, cmap, gradient, out, blocks, grads, ready, spread, packed, moved, terms, part, landed, total, mine,
    x_send, x_recv, a_send, a_recv, b_send, b_recv, g_send, g_recv, c_send, c_recv,
):
    me, rep = lax.axis_index("obs"), lax.axis_index("rep")
    width = total.shape[1]
    cap = moved.shape[2]
    barrier = pltpu.get_barrier_semaphore()
    for i in range(1, n):
        pl.semaphore_signal(barrier, inc=1, device_id={"obs": lax.rem(me + i, n)}, device_id_type=MESH)
    for i in range(1, m):
        pl.semaphore_signal(barrier, inc=1, device_id={"rep": lax.rem(rep + i, m)}, device_id_type=MESH)
    pack(counts, jac, res, ids, packed)
    part[...] = jnp.zeros_like(part)
    terms[...] = jnp.zeros_like(terms)
    pl.semaphore_wait(barrier, n + m - 2)

    def lanes_of(peer):
        return pl.ds(pl.multiple_of(peer * cap, cap), cap)

    def handing(i):
        peer = lax.rem(me + i, n)
        return pltpu.make_async_remote_copy(
            src_ref=packed.at[:, lanes_of(peer)],
            dst_ref=moved.at[i],
            send_sem=x_send.at[i],
            recv_sem=x_recv.at[i],
            device_id={"obs": peer},
            device_id_type=MESH,
        )

    def start(i, carry):
        handing(i).start()
        return carry

    def take(i, carry):
        handing(i).wait_recv()
        add_block(moved[i], terms, part)
        return carry

    def drain(i, carry):
        handing(i).wait_send()
        return carry

    lax.fori_loop(1, n, start, 0)
    add_block(packed[:, lanes_of(me)], terms, part)
    early = ready.shape[0] == n
    span = m * width

    def prepare(o, carry):
        ids_here = cmap[:, pl.ds(pl.multiple_of(o * span, span), span)]
        ready[o] = one_hot_of(lax.rem(ids_here, LOW), LOW)
        return carry

    if early:
        lax.fori_loop(0, n, prepare, 0)
    spread[...] = jnp.zeros_like(spread)
    lax.fori_loop(1, n, take, 0)

    def send(src, dst, s, r, axis, peer):
        copy = pltpu.make_async_remote_copy(
            src_ref=src, dst_ref=dst, send_sem=s, recv_sem=r, device_id={axis: peer}, device_id_type=MESH
        )
        copy.start()
        return copy

    first = []
    for i in range(1, m):
        peer = lax.rem(rep + i, m)
        first.append(send(part.at[peer], landed.at[i], a_send.at[i], a_recv.at[i], "rep", peer))
    lax.fori_loop(1, n, drain, 0)
    own = part[rep]
    for copy in first:
        copy.wait()
    for i in range(1, m):
        own = own + landed[i]
    total[...] = own[:KEPT]
    mine[...] = own[GRAD : GRAD + 9]
    grads[rep, me] = own[GRAD : GRAD + 9]
    blocks[rep] = own[:KEPT]
    around, wide, across = [], [], {}
    for i in range(1, n):
        peer = lax.rem(me + i, n)
        around.append(send(mine, grads.at[rep, me], g_send.at[i], g_recv.at[i], "obs", peer))
    for j in range(1, m):
        peer = lax.rem(rep + j, m)
        across[j, 0] = send(mine, grads.at[rep, me], c_send.at[j, 0], c_recv.at[j, 0], "rep", peer)
        wide.append(send(total, blocks.at[rep], b_send.at[j], b_recv.at[j], "rep", peer))
    for i in range(1, n):
        around[i - 1].wait_recv()
        source = lax.rem(me - i + n, n)
        for j in range(1, m):
            peer = lax.rem(rep + j, m)
            piece = grads.at[rep, source]
            across[j, i] = send(piece, piece, c_send.at[j, i], c_recv.at[j, i], "rep", peer)
    for copy in wide:
        copy.wait()
    expand(blocks, out)

    def settle(i, carry):
        source = lax.rem(me - i + n, n)
        for j in range(1, m):
            piece = grads.at[rep, source]
            pltpu.make_async_remote_copy(
                src_ref=piece, dst_ref=piece, send_sem=c_send.at[j, i], recv_sem=c_recv.at[j, i],
                device_id={"rep": lax.rem(rep + j, m)}, device_id_type=MESH,
            ).wait_recv()
        place_chunk(source, grads, cmap, ready if early else None, spread)
        return carry

    lax.fori_loop(0, n, settle, 0)
    lay_out(spread, gradient)
    for copy in around:
        copy.wait_send()
    for copy in across.values():
        copy.wait_send()


def write_kernel(gradient, blocks, gradient_out, blocks_out, gradient_sem, blocks_sem):
    first = pltpu.make_async_copy(gradient, gradient_out, gradient_sem)
    second = pltpu.make_async_copy(blocks, blocks_out, blocks_sem)
    first.start()
    second.start()
    first.wait()
    second.wait()


def local(jacobians, residuals, camera_local, bucket_counts, camera_map):
    n, m = lax.axis_size("obs"), lax.axis_size("rep")
    slots = jacobians.shape[1]
    cap = slots // n
    cams = camera_map.shape[0]
    width = CAM_DEV // m
    highs = cams // LOW
    dma = pltpu.SemaphoreType.DMA
    early = n if n * LOW * CAM_DEV * 2 <= 8 * 1024 * 1024 else 1
    limit = (24 if early == n else 60) * 1024 * 1024
    gradient, out = pl.pallas_call(
        functools.partial(main_kernel, n, m),
        out_shape=(jax.ShapeDtypeStruct((9, cams), F32), jax.ShapeDtypeStruct((81, CAM_DEV), F32)),
        in_specs=[pl.BlockSpec(memory_space=pltpu.SMEM)] + [vspec()] * 4,
        out_specs=(vspec(), vspec()),
        scratch_shapes=[
            VMEM((m, KEPT, width), F32),
            VMEM((m, n, 9, width), F32),
            VMEM((early, LOW, CAM_DEV), BF16),
            VMEM((highs * 18, LOW), F32),
            VMEM((21, slots), F32),
            VMEM((n, 21, cap), F32),
            VMEM((ROWS, cap), F32),
            VMEM((m, ROWS, width), F32),
            VMEM((m, ROWS, width), F32),
            VMEM((KEPT, width), F32),
            VMEM((9, width), F32),
            dma((n,)),
            dma((n,)),
            dma((m,)),
            dma((m,)),
            dma((m,)),
            dma((m,)),
            dma((n,)),
            dma((n,)),
            dma((m, n)),
            dma((m, n)),
        ],
        compiler_params=pltpu.CompilerParams(collective_id=0, has_side_effects=True, vmem_limit_bytes=limit),
    )(bucket_counts, jacobians, residuals, camera_local.reshape(1, slots), camera_map.reshape(1, cams))
    anywhere = pl.BlockSpec(memory_space=pl.ANY)
    shapes = (jax.ShapeDtypeStruct(gradient.shape, F32), jax.ShapeDtypeStruct(out.shape, F32))
    return pl.pallas_call(
        write_kernel,
        out_shape=shapes,
        in_specs=[anywhere] * 2,
        out_specs=(anywhere, anywhere),
        scratch_shapes=[dma, dma],
        compiler_params=pltpu.CompilerParams(vmem_limit_bytes=limit),
    )(gradient, out)


def solution(mesh):
    in_specs = (
        P(None, ("obs", "rep")),
        P(None, ("obs", "rep")),
        P(("obs", "rep")),
        P(("obs", "rep"), None),
        P(),
    )
    out_specs = (P(), P(None, "obs"))
    return jax.shard_map(local, mesh=mesh, in_specs=in_specs, out_specs=out_specs, check_vma=False)
```

```python
import functools

import jax
import jax.numpy as jnp
from jax import lax
from jax.experimental import pallas as pl
from jax.experimental.pallas import tpu as pltpu
from jax.sharding import PartitionSpec as P

CAM_DEV = 1024
MESH = pl.DeviceIdType.MESH
F32 = jnp.float32
BF16 = jnp.bfloat16
VMEM = pltpu.VMEM
ROWS = 56
GRAD = 45
KEPT = 48
LOW = 256


def vspec():
    return pl.BlockSpec(memory_space=VMEM)


def split(value):
    high = value.astype(BF16).astype(F32)
    return high, value - high


def pack(counts, jac, res, ids, out):
    buckets = counts.shape[1]
    cap = jac.shape[1] // buckets
    out[0:18, :] = jac[...]
    out[18:20, :] = res[...]
    place = lax.broadcasted_iota(jnp.int32, (1, cap), 1)
    for d in range(buckets):
        lanes = slice(d * cap, (d + 1) * cap)
        out[20:21, lanes] = jnp.where(place < counts[0, d], ids[:, lanes], -1).astype(F32)


def one_hot_of(low, wide):
    shape = (wide, low.shape[1])
    rows = lax.broadcasted_iota(jnp.int32, shape, 0).astype(F32).astype(BF16)
    there = jnp.broadcast_to(low.astype(F32), shape).astype(BF16)
    return jnp.where(there == rows, jnp.ones(shape, BF16), jnp.zeros(shape, BF16))


def add_block(block, terms, acc):
    cap = block.shape[1]
    lead, trail, res = block[0:9], block[9:18], block[18:20]
    ids = block[20:21].astype(jnp.int32)
    at = 0
    for k in range(9):
        terms[at : at + 9 - k, :] = lead[k : k + 1] * lead[k:9] + trail[k : k + 1] * trail[k:9]
        at += 9 - k
    terms[GRAD : GRAD + 9, :] = lead * res[0:1] + trail * res[1:2]
    high, low = split(terms[...])
    both = jnp.concatenate([high, low], axis=0).astype(BF16)
    pieces, _, width = acc.shape
    up = jnp.where(ids < 0, -1, ids // width)
    down = ids - up * width
    one_hot = one_hot_of(down, width)
    up = jnp.broadcast_to(up.astype(F32), both.shape).astype(BF16)
    zero = jnp.zeros_like(both)
    lhs = jnp.concatenate([jnp.where(up == jnp.asarray(h, BF16), both, zero) for h in range(pieces)], axis=0)
    added = lax.dot_general(lhs, one_hot, (((1,), (1,)), ((), ())), preferred_element_type=F32)
    for h in range(pieces):
        at = h * 2 * ROWS
        acc[h] += added[at : at + ROWS] + added[at + ROWS : at + 2 * ROWS]


def expand(blocks, out):
    m, _, width = blocks.shape
    at = 0
    for k in range(9):
        for l in range(k, 9):
            for r in range(m):
                row = blocks[r, at : at + 1, :]
                lanes = slice(r * width, (r + 1) * width)
                out[k * 9 + l : k * 9 + l + 1, lanes] = row
                if l != k:
                    out[l * 9 + k : l * 9 + k + 1, lanes] = row
            at += 1


def place_chunk(o, grads, cmap, ready, acc):
    m, n, _, width = grads.shape
    span = m * width
    highs = n * span // LOW
    slots = jnp.concatenate([grads[r, o] for r in range(m)], axis=1)
    ids = cmap[:, pl.ds(pl.multiple_of(o * span, span), span)]
    up = ids // LOW
    one_hot = one_hot_of(lax.rem(ids, LOW), LOW) if ready is None else ready[o]
    high, low = split(slots)
    top = jnp.concatenate([high[0:8], low[0:8]], axis=0).astype(BF16)
    up16 = jnp.broadcast_to(up.astype(F32), (16, span)).astype(BF16)
    none = jnp.zeros_like(top)
    mask = up == lax.broadcasted_iota(jnp.int32, (highs, span), 0)
    last = jnp.concatenate([jnp.where(mask, high[8:9], 0.0), jnp.where(mask, low[8:9], 0.0)], axis=0).astype(BF16)
    dims = (((1,), (1,)), ((), ()))
    group = min(highs, 32)

    def tiles(start):
        return [jnp.where(up16 == jnp.asarray(start + h, F32).astype(BF16), top, none) for h in range(group)]

    if group == highs:
        lhs = jnp.concatenate(tiles(0) + [last], axis=0)
        acc[...] += lax.dot_general(lhs, one_hot, dims, preferred_element_type=F32)
        return

    def some(g, carry):
        lhs = jnp.concatenate(tiles(g * group), axis=0)
        where = pl.ds(pl.multiple_of(g * group * 16, group * 16), group * 16)
        acc[where, :] += lax.dot_general(lhs, one_hot, dims, preferred_element_type=F32)
        return carry

    lax.fori_loop(0, highs // group, some, 0)
    acc[highs * 16 :, :] += lax.dot_general(last, one_hot, dims, preferred_element_type=F32)


def lay_out(acc, gradient):
    highs = gradient.shape[1] // LOW
    for h in range(highs):
        lanes = slice(h * LOW, (h + 1) * LOW)
        gradient[0:8, lanes] = acc[h * 16 : h * 16 + 8, :] + acc[h * 16 + 8 : h * 16 + 16, :]
        ninth = highs * 16 + h
        gradient[8:9, lanes] = acc[ninth : ninth + 1, :] + acc[ninth + highs : ninth + highs + 1, :]


def main_kernel(
    n, m, counts, jac_in, res_in, ids_in, cmap_in, gradient, out, jac, res, ids, cmap, load_sem, blocks, grads, ready, spread, packed, moved, terms, part, landed, total, mine,
    x_send, x_recv, a_send, a_recv, b_send, b_recv, g_send, g_recv, c_send, c_recv,
):
    me, rep = lax.axis_index("obs"), lax.axis_index("rep")
    width = total.shape[1]
    cap = moved.shape[2]
    barrier = pltpu.get_barrier_semaphore()
    for i in range(1, n):
        pl.semaphore_signal(barrier, inc=1, device_id={"obs": lax.rem(me + i, n)}, device_id_type=MESH)
    for i in range(1, m):
        pl.semaphore_signal(barrier, inc=1, device_id={"rep": lax.rem(rep + i, m)}, device_id_type=MESH)
    pairs = ((jac_in, jac), (res_in, res), (ids_in, ids), (cmap_in, cmap))
    loads = [pltpu.make_async_copy(src, dst, load_sem.at[k]) for k, (src, dst) in enumerate(pairs)]
    for load in loads:
        load.start()
    part[...] = jnp.zeros_like(part)
    terms[...] = jnp.zeros_like(terms)
    spread[...] = jnp.zeros_like(spread)
    for load in loads:
        load.wait()
    pack(counts, jac, res, ids, packed)
    pl.semaphore_wait(barrier, n + m - 2)

    def lanes_of(peer):
        return pl.ds(pl.multiple_of(peer * cap, cap), cap)

    def handing(i):
        peer = lax.rem(me + i, n)
        return pltpu.make_async_remote_copy(
            src_ref=packed.at[:, lanes_of(peer)],
            dst_ref=moved.at[i],
            send_sem=x_send.at[i],
            recv_sem=x_recv.at[i],
            device_id={"obs": peer},
            device_id_type=MESH,
        )

    def start(i, carry):
        handing(i).start()
        return carry

    def take(i, carry):
        handing(i).wait_recv()
        add_block(moved[i], terms, part)
        return carry

    def drain(i, carry):
        handing(i).wait_send()
        return carry

    lax.fori_loop(1, n, start, 0)
    add_block(packed[:, lanes_of(me)], terms, part)
    early = ready.shape[0] == n
    span = m * width

    def prepare(o, carry):
        ids_here = cmap[:, pl.ds(pl.multiple_of(o * span, span), span)]
        ready[o] = one_hot_of(lax.rem(ids_here, LOW), LOW)
        return carry

    if early:
        lax.fori_loop(0, n, prepare, 0)
    lax.fori_loop(1, n, take, 0)

    def send(src, dst, s, r, axis, peer):
        copy = pltpu.make_async_remote_copy(
            src_ref=src, dst_ref=dst, send_sem=s, recv_sem=r, device_id={axis: peer}, device_id_type=MESH
        )
        copy.start()
        return copy

    first = []
    for i in range(1, m):
        peer = lax.rem(rep + i, m)
        first.append(send(part.at[peer], landed.at[i], a_send.at[i], a_recv.at[i], "rep", peer))
    lax.fori_loop(1, n, drain, 0)
    own = part[rep]
    for copy in first:
        copy.wait()
    for i in range(1, m):
        own = own + landed[i]
    total[...] = own[:KEPT]
    mine[...] = own[GRAD : GRAD + 9]
    grads[rep, me] = own[GRAD : GRAD + 9]
    blocks[rep] = own[:KEPT]
    around, wide, across = [], [], {}
    for i in range(1, n):
        peer = lax.rem(me + i, n)
        around.append(send(mine, grads.at[rep, me], g_send.at[i], g_recv.at[i], "obs", peer))
    for j in range(1, m):
        peer = lax.rem(rep + j, m)
        across[j, 0] = send(mine, grads.at[rep, me], c_send.at[j, 0], c_recv.at[j, 0], "rep", peer)
        wide.append(send(total, blocks.at[rep], b_send.at[j], b_recv.at[j], "rep", peer))
    for i in range(1, n):
        around[i - 1].wait_recv()
        source = lax.rem(me - i + n, n)
        for j in range(1, m):
            peer = lax.rem(rep + j, m)
            piece = grads.at[rep, source]
            across[j, i] = send(piece, piece, c_send.at[j, i], c_recv.at[j, i], "rep", peer)
    for copy in wide:
        copy.wait()
    expand(blocks, out)

    def settle(i, carry):
        source = lax.rem(me - i + n, n)
        for j in range(1, m):
            piece = grads.at[rep, source]
            pltpu.make_async_remote_copy(
                src_ref=piece, dst_ref=piece, send_sem=c_send.at[j, i], recv_sem=c_recv.at[j, i],
                device_id={"rep": lax.rem(rep + j, m)}, device_id_type=MESH,
            ).wait_recv()
        place_chunk(source, grads, cmap, ready if early else None, spread)
        return carry

    lax.fori_loop(0, n, settle, 0)
    lay_out(spread, gradient)
    for copy in around:
        copy.wait_send()
    for copy in across.values():
        copy.wait_send()


def write_kernel(gradient, blocks, gradient_out, blocks_out, gradient_sem, blocks_sem):
    first = pltpu.make_async_copy(gradient, gradient_out, gradient_sem)
    second = pltpu.make_async_copy(blocks, blocks_out, blocks_sem)
    first.start()
    second.start()
    first.wait()
    second.wait()


def local(jacobians, residuals, camera_local, bucket_counts, camera_map):
    n, m = lax.axis_size("obs"), lax.axis_size("rep")
    slots = jacobians.shape[1]
    cap = slots // n
    cams = camera_map.shape[0]
    width = CAM_DEV // m
    highs = cams // LOW
    dma = pltpu.SemaphoreType.DMA
    early = n if n * LOW * CAM_DEV * 2 <= 8 * 1024 * 1024 else 1
    limit = (24 if early == n else 60) * 1024 * 1024
    gradient, out = pl.pallas_call(
        functools.partial(main_kernel, n, m),
        out_shape=(jax.ShapeDtypeStruct((9, cams), F32), jax.ShapeDtypeStruct((81, CAM_DEV), F32)),
        in_specs=[pl.BlockSpec(memory_space=pltpu.SMEM)] + [pl.BlockSpec(memory_space=pltpu.HBM)] * 4,
        out_specs=(vspec(), vspec()),
        scratch_shapes=[
            VMEM((18, slots), F32),
            VMEM((2, slots), F32),
            VMEM((1, slots), jnp.int32),
            VMEM((1, cams), jnp.int32),
            dma((4,)),
            VMEM((m, KEPT, width), F32),
            VMEM((m, n, 9, width), F32),
            VMEM((early, LOW, CAM_DEV), BF16),
            VMEM((highs * 18, LOW), F32),
            VMEM((21, slots), F32),
            VMEM((n, 21, cap), F32),
            VMEM((ROWS, cap), F32),
            VMEM((m, ROWS, width), F32),
            VMEM((m, ROWS, width), F32),
            VMEM((KEPT, width), F32),
            VMEM((9, width), F32),
            dma((n,)),
            dma((n,)),
            dma((m,)),
            dma((m,)),
            dma((m,)),
            dma((m,)),
            dma((n,)),
            dma((n,)),
            dma((m, n)),
            dma((m, n)),
        ],
        compiler_params=pltpu.CompilerParams(collective_id=0, has_side_effects=True, vmem_limit_bytes=limit),
    )(bucket_counts, jacobians, residuals, camera_local.reshape(1, slots), camera_map.reshape(1, cams))
    anywhere = pl.BlockSpec(memory_space=pl.ANY)
    shapes = (jax.ShapeDtypeStruct(gradient.shape, F32), jax.ShapeDtypeStruct(out.shape, F32))
    return pl.pallas_call(
        write_kernel,
        out_shape=shapes,
        in_specs=[anywhere] * 2,
        out_specs=(anywhere, anywhere),
        scratch_shapes=[dma, dma],
        compiler_params=pltpu.CompilerParams(vmem_limit_bytes=limit),
    )(gradient, out)


def solution(mesh):
    in_specs = (
        P(None, ("obs", "rep")),
        P(None, ("obs", "rep")),
        P(("obs", "rep")),
        P(("obs", "rep"), None),
        P(),
    )
    out_specs = (P(), P(None, "obs"))
    return jax.shard_map(local, mesh=mesh, in_specs=in_specs, out_specs=out_specs, check_vma=False)
```

```python
import functools

import jax
import jax.numpy as jnp
from jax import lax
from jax.experimental import pallas as pl
from jax.experimental.pallas import tpu as pltpu
from jax.sharding import PartitionSpec as P

CAM_DEV = 1024
MESH = pl.DeviceIdType.MESH
F32 = jnp.float32
BF16 = jnp.bfloat16
VMEM = pltpu.VMEM
ROWS = 56
GRAD = 45
KEPT = 48
LOW = 256


def vspec():
    return pl.BlockSpec(memory_space=VMEM)


def split(value):
    high = value.astype(BF16).astype(F32)
    return high, value - high


def pack(counts, jac, res, ids, out):
    buckets = counts.shape[1]
    cap = jac.shape[1] // buckets
    out[0:18, :] = jac[...]
    out[18:20, :] = res[...]
    place = lax.broadcasted_iota(jnp.int32, (1, cap), 1)
    for d in range(buckets):
        lanes = slice(d * cap, (d + 1) * cap)
        out[20:21, lanes] = jnp.where(place < counts[0, d], ids[:, lanes], -1).astype(F32)


def one_hot_of(low, wide):
    shape = (wide, low.shape[1])
    rows = lax.broadcasted_iota(jnp.int32, shape, 0).astype(F32).astype(BF16)
    there = jnp.broadcast_to(low.astype(F32), shape).astype(BF16)
    return jnp.where(there == rows, jnp.ones(shape, BF16), jnp.zeros(shape, BF16))


def add_block(block, terms, acc):
    cap = block.shape[1]
    lead, trail, res = block[0:9], block[9:18], block[18:20]
    ids = block[20:21].astype(jnp.int32)
    at = 0
    for k in range(9):
        terms[at : at + 9 - k, :] = lead[k : k + 1] * lead[k:9] + trail[k : k + 1] * trail[k:9]
        at += 9 - k
    terms[GRAD : GRAD + 9, :] = lead * res[0:1] + trail * res[1:2]
    high, low = split(terms[...])
    both = jnp.concatenate([high, low], axis=0).astype(BF16)
    pieces, _, width = acc.shape
    up = jnp.where(ids < 0, -1, ids // width)
    down = ids - up * width
    one_hot = one_hot_of(down, width)
    up = jnp.broadcast_to(up.astype(F32), both.shape).astype(BF16)
    zero = jnp.zeros_like(both)
    lhs = jnp.concatenate([jnp.where(up == jnp.asarray(h, BF16), both, zero) for h in range(pieces)], axis=0)
    added = lax.dot_general(lhs, one_hot, (((1,), (1,)), ((), ())), preferred_element_type=F32)
    for h in range(pieces):
        at = h * 2 * ROWS
        acc[h] += added[at : at + ROWS] + added[at + ROWS : at + 2 * ROWS]


def expand(blocks, out):
    m, _, width = blocks.shape
    at = 0
    for k in range(9):
        for l in range(k, 9):
            for r in range(m):
                row = blocks[r, at : at + 1, :]
                lanes = slice(r * width, (r + 1) * width)
                out[k * 9 + l : k * 9 + l + 1, lanes] = row
                if l != k:
                    out[l * 9 + k : l * 9 + k + 1, lanes] = row
            at += 1


def place_chunk(o, grads, cmap, ready, acc):
    m, n, _, width = grads.shape
    span = m * width
    highs = n * span // LOW
    slots = jnp.concatenate([grads[r, o] for r in range(m)], axis=1)
    ids = cmap[:, pl.ds(pl.multiple_of(o * span, span), span)]
    up = ids // LOW
    one_hot = one_hot_of(lax.rem(ids, LOW), LOW) if ready is None else ready[o]
    high, low = split(slots)
    top = jnp.concatenate([high[0:8], low[0:8]], axis=0).astype(BF16)
    up16 = jnp.broadcast_to(up.astype(F32), (16, span)).astype(BF16)
    none = jnp.zeros_like(top)
    mask = up == lax.broadcasted_iota(jnp.int32, (highs, span), 0)
    last = jnp.concatenate([jnp.where(mask, high[8:9], 0.0), jnp.where(mask, low[8:9], 0.0)], axis=0).astype(BF16)
    dims = (((1,), (1,)), ((), ()))
    group = min(highs, 32)

    def tiles(start):
        return [jnp.where(up16 == jnp.asarray(start + h, F32).astype(BF16), top, none) for h in range(group)]

    if group == highs:
        lhs = jnp.concatenate(tiles(0) + [last], axis=0)
        acc[...] += lax.dot_general(lhs, one_hot, dims, preferred_element_type=F32)
        return

    def some(g, carry):
        lhs = jnp.concatenate(tiles(g * group), axis=0)
        where = pl.ds(pl.multiple_of(g * group * 16, group * 16), group * 16)
        acc[where, :] += lax.dot_general(lhs, one_hot, dims, preferred_element_type=F32)
        return carry

    lax.fori_loop(0, highs // group, some, 0)
    acc[highs * 16 :, :] += lax.dot_general(last, one_hot, dims, preferred_element_type=F32)


def lay_out(acc, gradient):
    highs = gradient.shape[1] // LOW
    for h in range(highs):
        lanes = slice(h * LOW, (h + 1) * LOW)
        gradient[0:8, lanes] = acc[h * 16 : h * 16 + 8, :] + acc[h * 16 + 8 : h * 16 + 16, :]
        ninth = highs * 16 + h
        gradient[8:9, lanes] = acc[ninth : ninth + 1, :] + acc[ninth + highs : ninth + highs + 1, :]


def main_kernel(
    n, m, counts, jac_in, res_in, ids_in, cmap_in, gradient, out, jac, res, ids, cmap, load_sem, blocks, grads, ready, spread, packed, moved, terms, part, landed, total, mine,
    x_send, x_recv, a_send, a_recv, b_send, b_recv, g_send, g_recv, c_send, c_recv,
):
    me, rep = lax.axis_index("obs"), lax.axis_index("rep")
    width = total.shape[1]
    cap = moved.shape[2]
    barrier = pltpu.get_barrier_semaphore()
    for i in range(1, n):
        pl.semaphore_signal(barrier, inc=1, device_id={"obs": lax.rem(me + i, n)}, device_id_type=MESH)
    for i in range(1, m):
        pl.semaphore_signal(barrier, inc=1, device_id={"rep": lax.rem(rep + i, m)}, device_id_type=MESH)
    pairs = ((jac_in, jac), (res_in, res), (ids_in, ids), (cmap_in, cmap))
    loads = [pltpu.make_async_copy(src, dst, load_sem.at[k]) for k, (src, dst) in enumerate(pairs)]
    for load in loads:
        load.start()
    part[...] = jnp.zeros_like(part)
    terms[...] = jnp.zeros_like(terms)
    spread[...] = jnp.zeros_like(spread)
    for load in loads:
        load.wait()
    pack(counts, jac, res, ids, packed)
    pl.semaphore_wait(barrier, n + m - 2)

    def lanes_of(peer):
        return pl.ds(pl.multiple_of(peer * cap, cap), cap)

    def handing(i):
        peer = lax.rem(me + i, n)
        return pltpu.make_async_remote_copy(
            src_ref=packed.at[:, lanes_of(peer)],
            dst_ref=moved.at[i],
            send_sem=x_send.at[i],
            recv_sem=x_recv.at[i],
            device_id={"obs": peer},
            device_id_type=MESH,
        )

    def start(i, carry):
        handing(i).start()
        return carry

    def take(i, carry):
        handing(i).wait_recv()
        add_block(moved[i], terms, part)
        return carry

    def drain(i, carry):
        handing(i).wait_send()
        return carry

    lax.fori_loop(1, n, start, 0)
    add_block(packed[:, lanes_of(me)], terms, part)
    early = ready.shape[0] == n
    span = m * width

    def prepare(o, carry):
        ids_here = cmap[:, pl.ds(pl.multiple_of(o * span, span), span)]
        ready[o] = one_hot_of(lax.rem(ids_here, LOW), LOW)
        return carry

    if early:
        lax.fori_loop(0, n, prepare, 0)
    lax.fori_loop(1, n, take, 0)

    def send(src, dst, s, r, axis, peer):
        copy = pltpu.make_async_remote_copy(
            src_ref=src, dst_ref=dst, send_sem=s, recv_sem=r, device_id={axis: peer}, device_id_type=MESH
        )
        copy.start()
        return copy

    first = []
    for i in range(1, m):
        peer = lax.rem(rep + i, m)
        first.append(send(part.at[peer], landed.at[i], a_send.at[i], a_recv.at[i], "rep", peer))
    lax.fori_loop(1, n, drain, 0)
    own = part[rep]
    for copy in first:
        copy.wait()
    for i in range(1, m):
        own = own + landed[i]
    total[...] = own[:KEPT]
    mine[...] = own[GRAD : GRAD + 9]
    grads[rep, me] = own[GRAD : GRAD + 9]
    blocks[rep] = own[:KEPT]
    around, wide, across = [], [], {}
    for i in range(1, n):
        peer = lax.rem(me + i, n)
        around.append(send(mine, grads.at[rep, me], g_send.at[i], g_recv.at[i], "obs", peer))
    for j in range(1, m):
        peer = lax.rem(rep + j, m)
        across[j, 0] = send(mine, grads.at[rep, me], c_send.at[j, 0], c_recv.at[j, 0], "rep", peer)
        wide.append(send(total, blocks.at[rep], b_send.at[j], b_recv.at[j], "rep", peer))
    for i in range(1, n):
        around[i - 1].wait_recv()
        source = lax.rem(me - i + n, n)
        for j in range(1, m):
            peer = lax.rem(rep + j, m)
            piece = grads.at[rep, source]
            across[j, i] = send(piece, piece, c_send.at[j, i], c_recv.at[j, i], "rep", peer)
    for copy in wide:
        copy.wait()
    expand(blocks, out)

    def settle(i, carry):
        source = lax.rem(me - i + n, n)
        for j in range(1, m):
            piece = grads.at[rep, source]
            pltpu.make_async_remote_copy(
                src_ref=piece, dst_ref=piece, send_sem=c_send.at[j, i], recv_sem=c_recv.at[j, i],
                device_id={"rep": lax.rem(rep + j, m)}, device_id_type=MESH,
            ).wait_recv()
        place_chunk(source, grads, cmap, ready if early else None, spread)
        return carry

    lax.fori_loop(0, n, settle, 0)
    lay_out(spread, gradient)
    for copy in around:
        copy.wait_send()
    for copy in across.values():
        copy.wait_send()


def write_kernel(gradient, blocks, gradient_out, blocks_out, gradient_held, blocks_held, in_sem, out_sem):
    def cut(ref, count):
        step = ref.shape[1] // count
        return [ref.at[:, pl.ds(c * step, step)] for c in range(count)]

    jobs = list(zip(cut(blocks, 2), cut(blocks_held, 2), cut(blocks_out, 2)))
    jobs += list(zip(cut(gradient, 4), cut(gradient_held, 4), cut(gradient_out, 4)))
    reads = [pltpu.make_async_copy(job[0], job[1], in_sem.at[j]) for j, job in enumerate(jobs)]
    writes = [pltpu.make_async_copy(job[1], job[2], out_sem.at[j]) for j, job in enumerate(jobs)]
    for read in reads:
        read.start()
    for read, write in zip(reads, writes):
        read.wait()
        write.start()
    for write in writes:
        write.wait()


def local(jacobians, residuals, camera_local, bucket_counts, camera_map):
    n, m = lax.axis_size("obs"), lax.axis_size("rep")
    slots = jacobians.shape[1]
    cap = slots // n
    cams = camera_map.shape[0]
    width = CAM_DEV // m
    highs = cams // LOW
    dma = pltpu.SemaphoreType.DMA
    early = n if n * LOW * CAM_DEV * 2 <= 8 * 1024 * 1024 else 1
    limit = 60 * 1024 * 1024
    gradient, out = pl.pallas_call(
        functools.partial(main_kernel, n, m),
        out_shape=(jax.ShapeDtypeStruct((9, cams), F32), jax.ShapeDtypeStruct((81, CAM_DEV), F32)),
        in_specs=[pl.BlockSpec(memory_space=pltpu.SMEM)] + [pl.BlockSpec(memory_space=pltpu.HBM)] * 4,
        out_specs=(vspec(), vspec()),
        scratch_shapes=[
            VMEM((18, slots), F32),
            VMEM((2, slots), F32),
            VMEM((1, slots), jnp.int32),
            VMEM((1, cams), jnp.int32),
            dma((4,)),
            VMEM((m, KEPT, width), F32),
            VMEM((m, n, 9, width), F32),
            VMEM((early, LOW, CAM_DEV), BF16),
            VMEM((highs * 18, LOW), F32),
            VMEM((21, slots), F32),
            VMEM((n, 21, cap), F32),
            VMEM((ROWS, cap), F32),
            VMEM((m, ROWS, width), F32),
            VMEM((m, ROWS, width), F32),
            VMEM((KEPT, width), F32),
            VMEM((9, width), F32),
            dma((n,)),
            dma((n,)),
            dma((m,)),
            dma((m,)),
            dma((m,)),
            dma((m,)),
            dma((n,)),
            dma((n,)),
            dma((m, n)),
            dma((m, n)),
        ],
        compiler_params=pltpu.CompilerParams(collective_id=0, has_side_effects=True, vmem_limit_bytes=limit),
    )(bucket_counts, jacobians, residuals, camera_local.reshape(1, slots), camera_map.reshape(1, cams))
    anywhere = pl.BlockSpec(memory_space=pl.ANY)
    shapes = (jax.ShapeDtypeStruct(gradient.shape, F32), jax.ShapeDtypeStruct(out.shape, F32))
    return pl.pallas_call(
        write_kernel,
        out_shape=shapes,
        in_specs=[anywhere] * 2,
        out_specs=(anywhere, anywhere),
        scratch_shapes=[VMEM(gradient.shape, F32), VMEM(out.shape, F32), dma((6,)), dma((6,))],
        compiler_params=pltpu.CompilerParams(vmem_limit_bytes=limit),
    )(gradient, out)


def solution(mesh):
    in_specs = (
        P(None, ("obs", "rep")),
        P(None, ("obs", "rep")),
        P(("obs", "rep")),
        P(("obs", "rep"), None),
        P(),
    )
    out_specs = (P(), P(None, "obs"))
    return jax.shard_map(local, mesh=mesh, in_specs=in_specs, out_specs=out_specs, check_vma=False)
```

```python
import functools

import jax
import jax.numpy as jnp
from jax import lax
from jax.experimental import pallas as pl
from jax.experimental.pallas import tpu as pltpu
from jax.sharding import PartitionSpec as P

CAM_DEV = 1024
MESH = pl.DeviceIdType.MESH
F32 = jnp.float32
BF16 = jnp.bfloat16
VMEM = pltpu.VMEM
ROWS = 56
HEAD = 16
KEPT = 48
LOW = 256


def vspec():
    return pl.BlockSpec(memory_space=VMEM)


def split(value):
    high = value.astype(BF16).astype(F32)
    return high, value - high


def pack(counts, jac, res, ids, out):
    buckets = counts.shape[1]
    cap = jac.shape[1] // buckets
    out[0:18, :] = jac[...]
    out[18:20, :] = res[...]
    place = lax.broadcasted_iota(jnp.int32, (1, cap), 1)
    for d in range(buckets):
        lanes = slice(d * cap, (d + 1) * cap)
        out[20:21, lanes] = jnp.where(place < counts[0, d], ids[:, lanes], -1).astype(F32)


def one_hot_of(low, wide):
    shape = (wide, low.shape[1])
    rows = lax.broadcasted_iota(jnp.int32, shape, 0).astype(F32).astype(BF16)
    there = jnp.broadcast_to(low.astype(F32), shape).astype(BF16)
    return jnp.where(there == rows, jnp.ones(shape, BF16), jnp.zeros(shape, BF16))


def add_block(block, terms, acc):
    cap = block.shape[1]
    lead, trail, res = block[0:9], block[9:18], block[18:20]
    ids = block[20:21].astype(jnp.int32)
    at = 9
    for k in range(9):
        terms[at : at + 9 - k, :] = lead[k : k + 1] * lead[k:9] + trail[k : k + 1] * trail[k:9]
        at += 9 - k
    terms[0:9, :] = lead * res[0:1] + trail * res[1:2]
    high, low = split(terms[...])
    both = jnp.concatenate([high, low], axis=0).astype(BF16)
    pieces, _, width = acc.shape
    up = jnp.where(ids < 0, -1, ids // width)
    down = ids - up * width
    one_hot = one_hot_of(down, width)
    up = jnp.broadcast_to(up.astype(F32), both.shape).astype(BF16)
    zero = jnp.zeros_like(both)
    lhs = jnp.concatenate([jnp.where(up == jnp.asarray(h, BF16), both, zero) for h in range(pieces)], axis=0)
    added = lax.dot_general(lhs, one_hot, (((1,), (1,)), ((), ())), preferred_element_type=F32)
    for h in range(pieces):
        at = h * 2 * ROWS
        acc[h] += added[at : at + ROWS] + added[at + ROWS : at + 2 * ROWS]


def expand(blocks, out):
    m, _, width = blocks.shape
    at = 1
    for k in range(9):
        for l in range(k, 9):
            for r in range(m):
                row = blocks[r, at : at + 1, :]
                lanes = slice(r * width, (r + 1) * width)
                out[k * 9 + l : k * 9 + l + 1, lanes] = row
                if l != k:
                    out[l * 9 + k : l * 9 + k + 1, lanes] = row
            at += 1


def place_chunk(o, grads, cmap, ready, acc):
    m, n, _, width = grads.shape
    span = m * width
    highs = n * span // LOW
    slots = jnp.concatenate([grads[r, o] for r in range(m)], axis=1)
    ids = cmap[:, pl.ds(pl.multiple_of(o * span, span), span)]
    up = ids // LOW
    one_hot = one_hot_of(lax.rem(ids, LOW), LOW) if ready is None else ready[o]
    high, low = split(slots)
    top = jnp.concatenate([high[0:8], low[0:8]], axis=0).astype(BF16)
    up16 = jnp.broadcast_to(up.astype(F32), (16, span)).astype(BF16)
    none = jnp.zeros_like(top)
    mask = up == lax.broadcasted_iota(jnp.int32, (highs, span), 0)
    last = jnp.concatenate([jnp.where(mask, high[8:9], 0.0), jnp.where(mask, low[8:9], 0.0)], axis=0).astype(BF16)
    dims = (((1,), (1,)), ((), ()))
    group = min(highs, 32)

    def tiles(start):
        return [jnp.where(up16 == jnp.asarray(start + h, F32).astype(BF16), top, none) for h in range(group)]

    if group == highs:
        lhs = jnp.concatenate(tiles(0) + [last], axis=0)
        acc[...] += lax.dot_general(lhs, one_hot, dims, preferred_element_type=F32)
        return

    def some(g, carry):
        lhs = jnp.concatenate(tiles(g * group), axis=0)
        where = pl.ds(pl.multiple_of(g * group * 16, group * 16), group * 16)
        acc[where, :] += lax.dot_general(lhs, one_hot, dims, preferred_element_type=F32)
        return carry

    lax.fori_loop(0, highs // group, some, 0)
    acc[highs * 16 :, :] += lax.dot_general(last, one_hot, dims, preferred_element_type=F32)


def lay_out(acc, gradient):
    highs = gradient.shape[1] // LOW
    for h in range(highs):
        lanes = slice(h * LOW, (h + 1) * LOW)
        gradient[0:8, lanes] = acc[h * 16 : h * 16 + 8, :] + acc[h * 16 + 8 : h * 16 + 16, :]
        ninth = highs * 16 + h
        gradient[8:9, lanes] = acc[ninth : ninth + 1, :] + acc[ninth + highs : ninth + highs + 1, :]


def main_kernel(
    n, m, counts, jac_in, res_in, ids_in, cmap_in, gradient, out, jac, res, ids, cmap, load_sem, blocks, grads, ready, spread, packed, moved, terms, part, landed, total, mine,
    x_send, x_recv, a_send, a_recv, b_send, b_recv, g_send, g_recv, c_send, c_recv,
):
    me, rep = lax.axis_index("obs"), lax.axis_index("rep")
    width = total.shape[1]
    cap = moved.shape[2]
    barrier = pltpu.get_barrier_semaphore()
    for i in range(1, n):
        pl.semaphore_signal(barrier, inc=1, device_id={"obs": lax.rem(me + i, n)}, device_id_type=MESH)
    for i in range(1, m):
        pl.semaphore_signal(barrier, inc=1, device_id={"rep": lax.rem(rep + i, m)}, device_id_type=MESH)
    pairs = ((jac_in, jac), (res_in, res), (ids_in, ids), (cmap_in, cmap))
    loads = [pltpu.make_async_copy(src, dst, load_sem.at[k]) for k, (src, dst) in enumerate(pairs)]
    for load in loads:
        load.start()
    part[...] = jnp.zeros_like(part)
    terms[...] = jnp.zeros_like(terms)
    spread[...] = jnp.zeros_like(spread)
    for load in loads:
        load.wait()
    pack(counts, jac, res, ids, packed)
    pl.semaphore_wait(barrier, n + m - 2)

    def lanes_of(peer):
        return pl.ds(pl.multiple_of(peer * cap, cap), cap)

    def handing(i):
        peer = lax.rem(me + i, n)
        return pltpu.make_async_remote_copy(
            src_ref=packed.at[:, lanes_of(peer)],
            dst_ref=moved.at[i],
            send_sem=x_send.at[i],
            recv_sem=x_recv.at[i],
            device_id={"obs": peer},
            device_id_type=MESH,
        )

    def start(i, carry):
        handing(i).start()
        return carry

    def take(i, carry):
        handing(i).wait_recv()
        add_block(moved[i], terms, part)
        return carry

    def drain(i, carry):
        handing(i).wait_send()
        return carry

    lax.fori_loop(1, n, start, 0)
    add_block(packed[:, lanes_of(me)], terms, part)
    early = ready.shape[0] == n
    span = m * width

    def prepare(o, carry):
        ids_here = cmap[:, pl.ds(pl.multiple_of(o * span, span), span)]
        ready[o] = one_hot_of(lax.rem(ids_here, LOW), LOW)
        return carry

    if early:
        lax.fori_loop(0, n, prepare, 0)
    lax.fori_loop(1, n, take, 0)

    def send(src, dst, s, r, axis, peer):
        copy = pltpu.make_async_remote_copy(
            src_ref=src, dst_ref=dst, send_sem=s, recv_sem=r, device_id={axis: peer}, device_id_type=MESH
        )
        copy.start()
        return copy

    first, second = [], []
    for half, rows, copies in ((0, pl.ds(0, HEAD), first), (1, pl.ds(HEAD, ROWS - HEAD), second)):
        for i in range(1, m):
            peer = lax.rem(rep + i, m)
            copies.append(
                send(part.at[peer, rows], landed.at[i, rows], a_send.at[half, i], a_recv.at[half, i], "rep", peer)
            )
    for copy in first:
        copy.wait_recv()
    head = part[rep, 0:HEAD]
    for i in range(1, m):
        head = head + landed[i, 0:HEAD]
    mine[...] = head[0:9]
    grads[rep, me] = head[0:9]
    around, wide, across = [], [], {}
    for i in range(1, n):
        peer = lax.rem(me + i, n)
        around.append(send(mine, grads.at[rep, me], g_send.at[i], g_recv.at[i], "obs", peer))
    for j in range(1, m):
        peer = lax.rem(rep + j, m)
        across[j, 0] = send(mine, grads.at[rep, me], c_send.at[j, 0], c_recv.at[j, 0], "rep", peer)
    for copy in second:
        copy.wait_recv()
    rest = part[rep, ROWS - KEPT : ROWS]
    for i in range(1, m):
        rest = rest + landed[i, ROWS - KEPT : ROWS]
    total[...] = rest
    blocks[rep] = rest
    for j in range(1, m):
        peer = lax.rem(rep + j, m)
        wide.append(send(total, blocks.at[rep], b_send.at[j], b_recv.at[j], "rep", peer))
    for copy in first + second:
        copy.wait_send()
    lax.fori_loop(1, n, drain, 0)
    for i in range(1, n):
        around[i - 1].wait_recv()
        source = lax.rem(me - i + n, n)
        for j in range(1, m):
            peer = lax.rem(rep + j, m)
            piece = grads.at[rep, source]
            across[j, i] = send(piece, piece, c_send.at[j, i], c_recv.at[j, i], "rep", peer)
    for copy in wide:
        copy.wait()
    expand(blocks, out)

    def settle(i, carry):
        source = lax.rem(me - i + n, n)
        for j in range(1, m):
            piece = grads.at[rep, source]
            pltpu.make_async_remote_copy(
                src_ref=piece, dst_ref=piece, send_sem=c_send.at[j, i], recv_sem=c_recv.at[j, i],
                device_id={"rep": lax.rem(rep + j, m)}, device_id_type=MESH,
            ).wait_recv()
        place_chunk(source, grads, cmap, ready if early else None, spread)
        return carry

    lax.fori_loop(0, n, settle, 0)
    lay_out(spread, gradient)
    for copy in around:
        copy.wait_send()
    for copy in across.values():
        copy.wait_send()


def write_kernel(gradient, blocks, gradient_out, blocks_out, gradient_held, blocks_held, in_sem, out_sem):
    def cut(ref, count):
        step = ref.shape[1] // count
        return [ref.at[:, pl.ds(c * step, step)] for c in range(count)]

    jobs = list(zip(cut(blocks, 2), cut(blocks_held, 2), cut(blocks_out, 2)))
    jobs += list(zip(cut(gradient, 4), cut(gradient_held, 4), cut(gradient_out, 4)))
    reads = [pltpu.make_async_copy(job[0], job[1], in_sem.at[j]) for j, job in enumerate(jobs)]
    writes = [pltpu.make_async_copy(job[1], job[2], out_sem.at[j]) for j, job in enumerate(jobs)]
    for read in reads:
        read.start()
    for read, write in zip(reads, writes):
        read.wait()
        write.start()
    for write in writes:
        write.wait()


def local(jacobians, residuals, camera_local, bucket_counts, camera_map):
    n, m = lax.axis_size("obs"), lax.axis_size("rep")
    slots = jacobians.shape[1]
    cap = slots // n
    cams = camera_map.shape[0]
    width = CAM_DEV // m
    highs = cams // LOW
    dma = pltpu.SemaphoreType.DMA
    early = n if n * LOW * CAM_DEV * 2 <= 8 * 1024 * 1024 else 1
    limit = 60 * 1024 * 1024
    gradient, out = pl.pallas_call(
        functools.partial(main_kernel, n, m),
        out_shape=(jax.ShapeDtypeStruct((9, cams), F32), jax.ShapeDtypeStruct((81, CAM_DEV), F32)),
        in_specs=[pl.BlockSpec(memory_space=pltpu.SMEM)] + [pl.BlockSpec(memory_space=pltpu.HBM)] * 4,
        out_specs=(vspec(), vspec()),
        scratch_shapes=[
            VMEM((18, slots), F32),
            VMEM((2, slots), F32),
            VMEM((1, slots), jnp.int32),
            VMEM((1, cams), jnp.int32),
            dma((4,)),
            VMEM((m, KEPT, width), F32),
            VMEM((m, n, 9, width), F32),
            VMEM((early, LOW, CAM_DEV), BF16),
            VMEM((highs * 18, LOW), F32),
            VMEM((21, slots), F32),
            VMEM((n, 21, cap), F32),
            VMEM((ROWS, cap), F32),
            VMEM((m, ROWS, width), F32),
            VMEM((m, ROWS, width), F32),
            VMEM((KEPT, width), F32),
            VMEM((9, width), F32),
            dma((n,)),
            dma((n,)),
            dma((2, m)),
            dma((2, m)),
            dma((m,)),
            dma((m,)),
            dma((n,)),
            dma((n,)),
            dma((m, n)),
            dma((m, n)),
        ],
        compiler_params=pltpu.CompilerParams(collective_id=0, has_side_effects=True, vmem_limit_bytes=limit),
    )(bucket_counts, jacobians, residuals, camera_local.reshape(1, slots), camera_map.reshape(1, cams))
    anywhere = pl.BlockSpec(memory_space=pl.ANY)
    shapes = (jax.ShapeDtypeStruct(gradient.shape, F32), jax.ShapeDtypeStruct(out.shape, F32))
    return pl.pallas_call(
        write_kernel,
        out_shape=shapes,
        in_specs=[anywhere] * 2,
        out_specs=(anywhere, anywhere),
        scratch_shapes=[VMEM(gradient.shape, F32), VMEM(out.shape, F32), dma((6,)), dma((6,))],
        compiler_params=pltpu.CompilerParams(vmem_limit_bytes=limit),
    )(gradient, out)


def solution(mesh):
    in_specs = (
        P(None, ("obs", "rep")),
        P(None, ("obs", "rep")),
        P(("obs", "rep")),
        P(("obs", "rep"), None),
        P(),
    )
    out_specs = (P(), P(None, "obs"))
    return jax.shard_map(local, mesh=mesh, in_specs=in_specs, out_specs=out_specs, check_vma=False)
```

```python
import functools

import jax
import jax.numpy as jnp
from jax import lax
from jax.experimental import pallas as pl
from jax.experimental.pallas import tpu as pltpu
from jax.sharding import PartitionSpec as P

CAM_DEV = 1024
MESH = pl.DeviceIdType.MESH
F32 = jnp.float32
BF16 = jnp.bfloat16
VMEM = pltpu.VMEM
ROWS = 56
HEAD = 16
KEPT = 48
LOW = 256


def vspec():
    return pl.BlockSpec(memory_space=VMEM)


def split(value):
    high = value.astype(BF16).astype(F32)
    return high, value - high


def pack(counts, jac, res, ids, out):
    buckets = counts.shape[1]
    cap = jac.shape[1] // buckets
    out[0:18, :] = jac[...]
    out[18:20, :] = res[...]
    place = lax.broadcasted_iota(jnp.int32, (1, cap), 1)
    for d in range(buckets):
        lanes = slice(d * cap, (d + 1) * cap)
        out[20:21, lanes] = jnp.where(place < counts[0, d], ids[:, lanes], -1).astype(F32)


def one_hot_of(low, wide):
    shape = (wide, low.shape[1])
    rows = lax.broadcasted_iota(jnp.int32, shape, 0).astype(F32).astype(BF16)
    there = jnp.broadcast_to(low.astype(F32), shape).astype(BF16)
    return jnp.where(there == rows, jnp.ones(shape, BF16), jnp.zeros(shape, BF16))


def add_block(block, terms, acc):
    cap = block.shape[1]
    lead, trail, res = block[0:9], block[9:18], block[18:20]
    ids = block[20:21].astype(jnp.int32)
    at = 9
    for k in range(9):
        terms[at : at + 9 - k, :] = lead[k : k + 1] * lead[k:9] + trail[k : k + 1] * trail[k:9]
        at += 9 - k
    terms[0:9, :] = lead * res[0:1] + trail * res[1:2]
    high, low = split(terms[...])
    both = jnp.concatenate([high, low], axis=0).astype(BF16)
    pieces, _, width = acc.shape
    up = jnp.where(ids < 0, -1, ids // width)
    down = ids - up * width
    one_hot = one_hot_of(down, width)
    up = jnp.broadcast_to(up.astype(F32), both.shape).astype(BF16)
    zero = jnp.zeros_like(both)
    lhs = jnp.concatenate([jnp.where(up == jnp.asarray(h, BF16), both, zero) for h in range(pieces)], axis=0)
    added = lax.dot_general(lhs, one_hot, (((1,), (1,)), ((), ())), preferred_element_type=F32)
    for h in range(pieces):
        at = h * 2 * ROWS
        acc[h] += added[at : at + ROWS] + added[at + ROWS : at + 2 * ROWS]


def expand(blocks, out):
    m, _, width = blocks.shape
    at = 1
    for k in range(9):
        for l in range(k, 9):
            for r in range(m):
                row = blocks[r, at : at + 1, :]
                lanes = slice(r * width, (r + 1) * width)
                out[k * 9 + l : k * 9 + l + 1, lanes] = row
                if l != k:
                    out[l * 9 + k : l * 9 + k + 1, lanes] = row
            at += 1


def place_chunk(o, grads, cmap, ready, acc):
    m, n, _, width = grads.shape
    span = m * width
    highs = n * span // LOW
    slots = jnp.concatenate([grads[r, o] for r in range(m)], axis=1)
    ids = cmap[:, pl.ds(pl.multiple_of(o * span, span), span)]
    up = ids // LOW
    one_hot = one_hot_of(lax.rem(ids, LOW), LOW) if ready is None else ready[o]
    high, low = split(slots)
    top = jnp.concatenate([high[0:8], low[0:8]], axis=0).astype(BF16)
    up16 = jnp.broadcast_to(up.astype(F32), (16, span)).astype(BF16)
    none = jnp.zeros_like(top)
    mask = up == lax.broadcasted_iota(jnp.int32, (highs, span), 0)
    last = jnp.concatenate([jnp.where(mask, high[8:9], 0.0), jnp.where(mask, low[8:9], 0.0)], axis=0).astype(BF16)
    dims = (((1,), (1,)), ((), ()))
    group = min(highs, 32)

    def tiles(start):
        return [jnp.where(up16 == jnp.asarray(start + h, F32).astype(BF16), top, none) for h in range(group)]

    if group == highs:
        lhs = jnp.concatenate(tiles(0) + [last], axis=0)
        acc[...] += lax.dot_general(lhs, one_hot, dims, preferred_element_type=F32)
        return

    def some(g, carry):
        lhs = jnp.concatenate(tiles(g * group), axis=0)
        where = pl.ds(pl.multiple_of(g * group * 16, group * 16), group * 16)
        acc[where, :] += lax.dot_general(lhs, one_hot, dims, preferred_element_type=F32)
        return carry

    lax.fori_loop(0, highs // group, some, 0)
    acc[highs * 16 :, :] += lax.dot_general(last, one_hot, dims, preferred_element_type=F32)


def lay_out(acc, gradient):
    highs = gradient.shape[1] // LOW
    for h in range(highs):
        lanes = slice(h * LOW, (h + 1) * LOW)
        gradient[0:8, lanes] = acc[h * 16 : h * 16 + 8, :] + acc[h * 16 + 8 : h * 16 + 16, :]
        ninth = highs * 16 + h
        gradient[8:9, lanes] = acc[ninth : ninth + 1, :] + acc[ninth + highs : ninth + highs + 1, :]


def main_kernel(
    n, m, counts, jac_in, res_in, ids_in, cmap_in, gradient, out, jac, res, ids, cmap, load_sem, blocks, grads, ready, spread, packed, moved, terms, part, landed, total, mine,
    x_send, x_recv, a_send, a_recv, b_send, b_recv, g_send, g_recv, c_send, c_recv,
):
    me, rep = lax.axis_index("obs"), lax.axis_index("rep")
    width = total.shape[1]
    cap = moved.shape[2]
    barrier = pltpu.get_barrier_semaphore()
    for i in range(1, n):
        pl.semaphore_signal(barrier, inc=1, device_id={"obs": lax.rem(me + i, n)}, device_id_type=MESH)
    for i in range(1, m):
        pl.semaphore_signal(barrier, inc=1, device_id={"rep": lax.rem(rep + i, m)}, device_id_type=MESH)
    pairs = ((jac_in, jac), (res_in, res), (ids_in, ids), (cmap_in, cmap))
    loads = [pltpu.make_async_copy(src, dst, load_sem.at[k]) for k, (src, dst) in enumerate(pairs)]
    for load in loads:
        load.start()
    part[...] = jnp.zeros_like(part)
    terms[...] = jnp.zeros_like(terms)
    spread[...] = jnp.zeros_like(spread)
    for load in loads:
        load.wait()
    pack(counts, jac, res, ids, packed)
    pl.semaphore_wait(barrier, n + m - 2)

    def lanes_of(peer):
        return pl.ds(pl.multiple_of(peer * cap, cap), cap)

    def handing(i):
        peer = lax.rem(me + i, n)
        return pltpu.make_async_remote_copy(
            src_ref=packed.at[:, lanes_of(peer)],
            dst_ref=moved.at[i],
            send_sem=x_send.at[i],
            recv_sem=x_recv.at[i],
            device_id={"obs": peer},
            device_id_type=MESH,
        )

    def start(i, carry):
        handing(i).start()
        return carry

    def take(i, carry):
        handing(i).wait_recv()
        add_block(moved[i], terms, part)
        return carry

    def drain(i, carry):
        handing(i).wait_send()
        return carry

    lax.fori_loop(1, n, start, 0)
    add_block(packed[:, lanes_of(me)], terms, part)
    early = ready.shape[0] == n
    span = m * width

    def prepare(o, carry):
        ids_here = cmap[:, pl.ds(pl.multiple_of(o * span, span), span)]
        ready[o] = one_hot_of(lax.rem(ids_here, LOW), LOW)
        return carry

    if early:
        lax.fori_loop(0, n, prepare, 0)
    lax.fori_loop(1, n, take, 0)

    def send(src, dst, s, r, axis, peer):
        copy = pltpu.make_async_remote_copy(
            src_ref=src, dst_ref=dst, send_sem=s, recv_sem=r, device_id={axis: peer}, device_id_type=MESH
        )
        copy.start()
        return copy

    first, second = [], []
    for half, rows, copies in ((0, pl.ds(0, HEAD), first), (1, pl.ds(HEAD, ROWS - HEAD), second)):
        for i in range(1, m):
            peer = lax.rem(rep + i, m)
            copies.append(
                send(part.at[peer, rows], landed.at[i, rows], a_send.at[half, i], a_recv.at[half, i], "rep", peer)
            )
    for copy in first:
        copy.wait_recv()
    head = part[rep, 0:HEAD]
    for i in range(1, m):
        head = head + landed[i, 0:HEAD]
    mine[...] = head[0:9]
    grads[rep, me] = head[0:9]
    around, wide, across = [], [], {}
    for i in range(1, n):
        peer = lax.rem(me + i, n)
        around.append(send(mine, grads.at[rep, me], g_send.at[i], g_recv.at[i], "obs", peer))
    for j in range(1, m):
        peer = lax.rem(rep + j, m)
        across[j, 0] = send(mine, grads.at[rep, me], c_send.at[j, 0], c_recv.at[j, 0], "rep", peer)
    for copy in second:
        copy.wait_recv()
    rest = part[rep, ROWS - KEPT : ROWS]
    for i in range(1, m):
        rest = rest + landed[i, ROWS - KEPT : ROWS]
    total[...] = rest
    blocks[rep] = rest
    for j in range(1, m):
        peer = lax.rem(rep + j, m)
        wide.append(send(total, blocks.at[rep], b_send.at[j], b_recv.at[j], "rep", peer))
    for copy in first + second:
        copy.wait_send()
    lax.fori_loop(1, n, drain, 0)
    for i in range(1, n):
        around[i - 1].wait_recv()
        source = lax.rem(me - i + n, n)
        for j in range(1, m):
            peer = lax.rem(rep + j, m)
            piece = grads.at[rep, source]
            across[j, i] = send(piece, piece, c_send.at[j, i], c_recv.at[j, i], "rep", peer)
    for copy in wide:
        copy.wait()
    expand(blocks, out)

    def settle(i, carry):
        source = lax.rem(me - i + n, n)
        for j in range(1, m):
            piece = grads.at[rep, source]
            pltpu.make_async_remote_copy(
                src_ref=piece, dst_ref=piece, send_sem=c_send.at[j, i], recv_sem=c_recv.at[j, i],
                device_id={"rep": lax.rem(rep + j, m)}, device_id_type=MESH,
            ).wait_recv()
        place_chunk(source, grads, cmap, ready if early else None, spread)
        return carry

    lax.fori_loop(0, n, settle, 0, unroll=2)
    lay_out(spread, gradient)
    for copy in around:
        copy.wait_send()
    for copy in across.values():
        copy.wait_send()


def write_kernel(gradient, blocks, gradient_out, blocks_out, gradient_held, blocks_held, in_sem, out_sem):
    def cut(ref, count):
        step = ref.shape[1] // count
        return [ref.at[:, pl.ds(c * step, step)] for c in range(count)]

    jobs = list(zip(cut(blocks, 2), cut(blocks_held, 2), cut(blocks_out, 2)))
    jobs += list(zip(cut(gradient, 4), cut(gradient_held, 4), cut(gradient_out, 4)))
    reads = [pltpu.make_async_copy(job[0], job[1], in_sem.at[j]) for j, job in enumerate(jobs)]
    writes = [pltpu.make_async_copy(job[1], job[2], out_sem.at[j]) for j, job in enumerate(jobs)]
    for read in reads:
        read.start()
    for read, write in zip(reads, writes):
        read.wait()
        write.start()
    for write in writes:
        write.wait()


def local(jacobians, residuals, camera_local, bucket_counts, camera_map):
    n, m = lax.axis_size("obs"), lax.axis_size("rep")
    slots = jacobians.shape[1]
    cap = slots // n
    cams = camera_map.shape[0]
    width = CAM_DEV // m
    highs = cams // LOW
    dma = pltpu.SemaphoreType.DMA
    early = n if n * LOW * CAM_DEV * 2 <= 8 * 1024 * 1024 else 1
    limit = 60 * 1024 * 1024
    gradient, out = pl.pallas_call(
        functools.partial(main_kernel, n, m),
        out_shape=(jax.ShapeDtypeStruct((9, cams), F32), jax.ShapeDtypeStruct((81, CAM_DEV), F32)),
        in_specs=[pl.BlockSpec(memory_space=pltpu.SMEM)] + [pl.BlockSpec(memory_space=pltpu.HBM)] * 4,
        out_specs=(vspec(), vspec()),
        scratch_shapes=[
            VMEM((18, slots), F32),
            VMEM((2, slots), F32),
            VMEM((1, slots), jnp.int32),
            VMEM((1, cams), jnp.int32),
            dma((4,)),
            VMEM((m, KEPT, width), F32),
            VMEM((m, n, 9, width), F32),
            VMEM((early, LOW, CAM_DEV), BF16),
            VMEM((highs * 18, LOW), F32),
            VMEM((21, slots), F32),
            VMEM((n, 21, cap), F32),
            VMEM((ROWS, cap), F32),
            VMEM((m, ROWS, width), F32),
            VMEM((m, ROWS, width), F32),
            VMEM((KEPT, width), F32),
            VMEM((9, width), F32),
            dma((n,)),
            dma((n,)),
            dma((2, m)),
            dma((2, m)),
            dma((m,)),
            dma((m,)),
            dma((n,)),
            dma((n,)),
            dma((m, n)),
            dma((m, n)),
        ],
        compiler_params=pltpu.CompilerParams(collective_id=0, has_side_effects=True, vmem_limit_bytes=limit),
    )(bucket_counts, jacobians, residuals, camera_local.reshape(1, slots), camera_map.reshape(1, cams))
    anywhere = pl.BlockSpec(memory_space=pl.ANY)
    shapes = (jax.ShapeDtypeStruct(gradient.shape, F32), jax.ShapeDtypeStruct(out.shape, F32))
    return pl.pallas_call(
        write_kernel,
        out_shape=shapes,
        in_specs=[anywhere] * 2,
        out_specs=(anywhere, anywhere),
        scratch_shapes=[VMEM(gradient.shape, F32), VMEM(out.shape, F32), dma((6,)), dma((6,))],
        compiler_params=pltpu.CompilerParams(vmem_limit_bytes=limit),
    )(gradient, out)


def solution(mesh):
    in_specs = (
        P(None, ("obs", "rep")),
        P(None, ("obs", "rep")),
        P(("obs", "rep")),
        P(("obs", "rep"), None),
        P(),
    )
    out_specs = (P(), P(None, "obs"))
    return jax.shard_map(local, mesh=mesh, in_specs=in_specs, out_specs=out_specs, check_vma=False)
```
